32 devices in a mesh: dp: 8 (over z, y), tensor: 4 (over x, core).
Axes of the slice: x: 2, y: 2, z: 4, core: 2. Of those that a mesh axis runs over, the one named last changes fastest.
Arguments:
- layer_input: bfloat16 [4096, 2048], P(('dp', 'tensor')), may hold values from -6 to 6
- segment_ids: int32 [8, 512], P('dp'), may hold values from 0 to 2, never falling along the last dimension, each value on 1 to 256 neighbouring positions
- routes: int32 [4096, 6], P(('dp', 'tensor')), may hold values from 0 to 15, all different within a row
- route_weight: float32 [4096, 6], P(('dp', 'tensor')), may hold values from 0.1 to 1
- place_order: int32 [32, 768], P(('dp', 'tensor')), may hold values from 0 to 767, each once within a row
- attention_gain: bfloat16 [2048], P('dp'), may hold values from 0.099609375 to 1.8984375
- query_weight: bfloat16 [2048, 3072], P('dp', 'tensor'), may hold values from -0.125 to 0.125
- latent_weight: bfloat16 [2048, 576], P('dp'), may hold values from -0.125 to 0.125
- latent_gain: bfloat16 [512], P('dp'), may hold values from 0.099609375 to 1.8984375
- latent_up: bfloat16 [512, 4096], P('dp', 'tensor'), may hold values from -0.25 to 0.25
- output_weight: bfloat16 [2048, 2048], P('tensor', 'dp'), may hold values from -1 to 1
- experts_gain: bfloat16 [2048], P('dp'), may hold values from 0.099609375 to 1.8984375
- expert_gate: bfloat16 [16, 2048, 1408], P('dp', None, 'tensor'), may hold values from -0.125 to 0.125
- expert_up: bfloat16 [16, 2048, 1408], P('dp', None, 'tensor'), may hold values from -0.125 to 0.125
- expert_down: bfloat16 [16, 1408, 2048], P('dp', 'tensor'), may hold values from -0.15625 to 0.15625
- shared_gate: bfloat16 [2048, 2816], P('dp'), may hold values from -0.125 to 0.125
- shared_up: bfloat16 [2048, 2816], P('dp'), may hold values from -0.125 to 0.125
- shared_down: bfloat16 [2816, 2048], P(None, 'dp'), may hold values from -0.109375 to 0.109375
- out_cotangent: bfloat16 [4096, 2048], P(('dp', 'tensor')), may hold values from -6 to 6
Outputs:
- layer_output: bfloat16 [4096, 2048], P(('dp', 'tensor'))
- grad_input: float32 [4096, 2048], P(('dp', 'tensor'))
- grad_attention_gain: float32 [2048], P(('dp', 'tensor'))
- grad_query_weight: float32 [2048, 3072], P('dp', 'tensor')
- grad_latent_weight: float32 [2048, 576], P(('dp', 'tensor'))
- grad_latent_gain: float32 [512], P(('dp', 'tensor'))
- grad_latent_up: float32 [512, 4096], P('dp', 'tensor')
- grad_output_weight: float32 [2048, 2048], P('tensor', 'dp')
- grad_experts_gain: float32 [2048], P(('dp', 'tensor'))
- grad_expert_gate: float32 [16, 2048, 1408], P('dp', None, 'tensor')
- grad_expert_up: float32 [16, 2048, 1408], P('dp', None, 'tensor')
- grad_expert_down: float32 [16, 1408, 2048], P('dp', 'tensor')
- grad_shared_gate: float32 [2048, 2816], P('dp', 'tensor')
- grad_shared_up: float32 [2048, 2816], P('dp', 'tensor')
- grad_shared_down: float32 [2816, 2048], P('tensor', 'dp')
The draws below stay inside these ranges and needn't reach their ends.
Inputs may be any that keep to these rules, and one draw needn't show every extreme that they name: `routes`: each row names 6 different experts, and every expert is named by some row. `place_order`: each row holds every number from 0 to 767 once. `segment_ids`: document numbers never fall along a sequence; a document has 1 to 256 tokens.
All inputs are finite; a program needn't handle non-finite values.
Results may differ from the reference program's by a relative error of at most 0.02.
Values may be sent and summed in bfloat16 or wider, within the bound.
No kernel may reach another device: no remote copies, remote signals or barrier semaphores. Data moves between devices by JAX's collectives and lax.ppermute only.
A program may use at most 384 MiB of HBM per device.

```python
import math
import jax
import jax.numpy as jnp
import numpy as np
from jax import lax

D = 2048
HEADS = 16
QK_NOPE = 128
QK_ROPE = 64
V_DIM = 128
KV_RANK = 512
FF_EXP = 1408
FF_SHARED = 2816
TOPK = 6
TOK_DP = 512
SEQS = 8
TOKENS = 4096
TOK_SH = 128
SHARDS = 32
EXPERTS = 16
CAP = 60
N_TENSOR = 4


def block_levels(own_key, shape, cuts, smallest, largest):
    level, own = 1.0, jax.random.fold_in(own_key, 6)
    for axis_at, blocks in cuts:
        steps = jnp.exp(jax.random.uniform(jax.random.fold_in(own, axis_at), (blocks,), jnp.float32, smallest / len(cuts), largest / len(cuts)))
        level = level * jnp.repeat(steps, shape[axis_at] // blocks).reshape([-1 if axis == axis_at else 1 for axis in range(len(shape))])
    return level


def picks_of(own_key, rows, amount, top, lift):
    ranking = jax.random.permutation(jax.random.fold_in(own_key, 1), amount)
    pull = ranking
    for power in range(3):
        pull = pull * pull // amount
    pull = pull * lift // amount
    tickets = jax.random.randint(jax.random.fold_in(own_key, 2), (rows, amount), 0, 4096) + pull
    sure = jax.random.permutation(jax.random.fold_in(own_key, 3), rows)[jnp.arange(amount) % rows]
    tickets = jnp.where(jnp.arange(rows)[:, None] == sure[None, :], 1 << 14, tickets)
    merit = tickets * amount + jnp.arange(amount)
    return lax.top_k(merit.astype(jnp.int32), top)[1].astype(jnp.int32)


def split_up(count, total, most, slope):
    loads = [(1 << 20) // math.isqrt(rank ** slope) + 1 for rank in range(2, count + 1)]
    spare, counts = total - most - (count - 1), [1] * (count - 1)
    while spare > 0:
        movable = [i for i in range(count - 1) if counts[i] < most]
        mass, remaining = sum([loads[i] for i in movable]), spare
        for i in movable:
            extra = min(most - counts[i], max(1, remaining * loads[i] // mass), spare)
            counts[i] = counts[i] + extra
            spare = spare - extra
    return np.array([most] + counts)


def uneven_parts(own_key, number_of, total, bound, skew):
    if number_of == 2:
        one = jax.random.randint(own_key, (), max(1, total - bound), min(bound, total - 1) + 1)
        return jnp.stack([one, total - one])
    sizes = jnp.asarray(split_up(number_of, total, bound, skew), jnp.int32)
    twos = (number_of - 1) // 2
    source_of, taker = sizes[1:1 + 2 * twos:2], sizes[2:2 + 2 * twos:2]
    margin = jnp.minimum(source_of - 1, bound - taker)
    passed = jax.random.randint(jax.random.fold_in(own_key, 1), (twos,), 0, 1 << 20) % (margin + 1)
    sizes = sizes.at[1:1 + 2 * twos:2].set(source_of - passed).at[2:2 + 2 * twos:2].set(taker + passed)
    return sizes[jax.random.permutation(jax.random.fold_in(own_key, 2), number_of)]


def scatter_about(own_key, extent, width, bound, cuts=(), kind=jnp.bfloat16):
    values = width * jax.random.normal(own_key, extent, jnp.float32)
    if cuts:
        values = values * block_levels(own_key, extent, cuts, -0.22, 0.18)
    return jnp.clip(values, -bound, bound).astype(kind)


def setup_inputs(seed: int = 0) -> dict:
    key_of = jax.random.split(jax.random.key(seed), 20)
    layer_input = scatter_about(key_of[0], (TOKENS, D), 1.0, 6.0, ((0, 32),))
    segment_ids = jax.vmap(lambda own: jnp.searchsorted(jnp.cumsum(uneven_parts(own, 3, TOK_DP, TOK_DP // 2, 1)), jnp.arange(TOK_DP), side="right"))(jax.random.split(key_of[1], SEQS)).reshape((SEQS, TOK_DP)).astype(jnp.int32)
    routes = picks_of(key_of[2], TOKENS, EXPERTS, TOPK, 6144)
    route_weight = jnp.clip(jnp.exp(math.log(1.0) - 2.3025851 * jax.random.uniform(key_of[3], (TOKENS, TOPK), jnp.float32) ** block_levels(key_of[3], (TOKENS, TOPK), ((0, 32),), -0.2, 0.2)), 0.1, 1.0)
    place_order = jax.vmap(lambda own: jax.random.permutation(own, TOK_SH * TOPK))(jax.random.split(key_of[4], SHARDS)).reshape((SHARDS, TOK_SH * TOPK)).astype(jnp.int32)
    attention_gain = jnp.clip(1.0 + 0.18 * jax.random.normal(key_of[5], (D,), jnp.float32), 0.099609375, 1.8984375).astype(jnp.bfloat16)
    query_weight = scatter_about(key_of[6], (D, HEADS * (QK_NOPE + QK_ROPE)), D ** -0.5, 0.125, ((0, 8), (1, 4)))
    latent_weight = scatter_about(key_of[7], (D, KV_RANK + QK_ROPE), D ** -0.5, 0.125, ((0, 8),))
    latent_gain = jnp.clip(1.0 + 0.18 * jax.random.normal(key_of[8], (KV_RANK,), jnp.float32), 0.099609375, 1.8984375).astype(jnp.bfloat16)
    latent_up = scatter_about(key_of[9], (KV_RANK, HEADS * (QK_NOPE + V_DIM)), KV_RANK ** -0.5, 0.25, ((0, 8), (1, 4)))
    output_weight = scatter_about(key_of[10], (HEADS * V_DIM, D), (max(1, HEADS * V_DIM // 64)) ** -0.5, 1.0, ((0, 4), (1, 8)))
    experts_gain = jnp.clip(1.0 + 0.18 * jax.random.normal(key_of[11], (D,), jnp.float32), 0.099609375, 1.8984375).astype(jnp.bfloat16)
    expert_gate = scatter_about(key_of[12], (EXPERTS, D, FF_EXP), D ** -0.5, 0.125, ((0, 8), (2, 4)))
    expert_up = scatter_about(key_of[13], (EXPERTS, D, FF_EXP), D ** -0.5, 0.125, ((0, 8), (2, 4)))
    expert_down = scatter_about(key_of[14], (EXPERTS, FF_EXP, D), FF_EXP ** -0.5, 0.15625, ((0, 8), (1, 4)))
    shared_gate = scatter_about(key_of[15], (D, FF_SHARED), D ** -0.5, 0.125, ((0, 8),))
    shared_up = scatter_about(key_of[16], (D, FF_SHARED), D ** -0.5, 0.125, ((0, 8),))
    shared_down = scatter_about(key_of[17], (FF_SHARED, D), FF_SHARED ** -0.5, 0.109375, ((1, 8),))
    out_cotangent = scatter_about(key_of[18], (TOKENS, D), 1.0, 6.0, ((0, 32),))
    return dict(layer_input=layer_input, segment_ids=segment_ids, routes=routes, route_weight=route_weight, place_order=place_order, attention_gain=attention_gain, query_weight=query_weight, latent_weight=latent_weight, latent_gain=latent_gain, latent_up=latent_up, output_weight=output_weight, experts_gain=experts_gain, expert_gate=expert_gate, expert_up=expert_up, expert_down=expert_down, shared_gate=shared_gate, shared_up=shared_up, shared_down=shared_down, out_cotangent=out_cotangent)


NORM_EPS = 1e-06
PRECISE = lax.Precision.HIGHEST

@jax.custom_vjp
def low(v):
    return lax.optimization_barrier(v.astype(jnp.bfloat16)).astype(jnp.float32)

@jax.custom_vjp
def low_back(v):
    return v

def low_keep(v):
    return (low(v), None)

def low_pass(kept, grad):
    return (grad,)

def back_keep(v):
    return (v, None)

def back_low(kept, grad):
    return (low(grad),)
low.defvjp(low_keep, low_pass)
low_back.defvjp(back_keep, back_low)

def root_norm(values, gain_row):
    factor = lax.rsqrt(lax.optimization_barrier(jnp.mean(values * values, axis=-1, keepdims=True)) + NORM_EPS)
    return values * factor * gain_row

def turn_tables(positions, half_width):
    frequency = 10000.0 ** (-jnp.arange(half_width, dtype=jnp.float32) / half_width)
    angles = positions.astype(jnp.float32)[:, None] * frequency[None, :]
    return (jnp.cos(angles), jnp.sin(angles))

def rotate(values, cosine, sine_table):
    half_width = values.shape[-1] // 2
    first_half = values[..., :half_width]
    second_half = values[..., half_width:]
    return jnp.concatenate([first_half * cosine - second_half * sine_table, first_half * sine_table + second_half * cosine], axis=-1)

def silu_of(values):
    return values * jax.nn.sigmoid(values)

def slot_places(expert_ids, rank_order, expert_count):
    pair_count = expert_ids.shape[0]
    inverse = jnp.zeros((pair_count,), jnp.int32).at[rank_order].set(jnp.arange(pair_count, dtype=jnp.int32))
    ranked = expert_ids[inverse]
    onehot = (ranked[:, None] == jnp.arange(expert_count, dtype=jnp.int32)[None, :]).astype(jnp.int32)
    earlier = jnp.cumsum(onehot, axis=0) - onehot
    ranked_place = lax.optimization_barrier(jnp.sum(earlier * onehot, axis=1))
    return ranked_place[rank_order]

def reference(layer_input, segment_ids, routes, route_weight, place_order, attention_gain, query_weight, latent_weight, latent_gain, latent_up, output_weight, experts_gain, expert_gate, expert_up, expert_down, shared_gate, shared_up, shared_down, out_cotangent):
    pair_count = TOK_SH * TOPK
    slot_total = EXPERTS * SHARDS * CAP
    shard_routes = routes.reshape(SHARDS, pair_count)
    places = jax.vmap(lambda ids_row, order_row: slot_places(ids_row, order_row, EXPERTS))(shard_routes, place_order)
    kept_mask = places < CAP
    shard_ids = jnp.arange(SHARDS, dtype=jnp.int32)[:, None]
    slot_index = jnp.where(kept_mask, (shard_routes * SHARDS + shard_ids) * CAP + places, slot_total).reshape(-1)
    pair_tokens = (shard_ids * TOK_SH + jnp.arange(pair_count, dtype=jnp.int32)[None, :] // TOPK).reshape(-1)
    slot_tokens = jnp.full((slot_total,), TOKENS, jnp.int32).at[slot_index].set(pair_tokens, mode='drop').reshape(EXPERTS, SHARDS * CAP)
    slot_weights = jnp.zeros((slot_total,), jnp.float32).at[slot_index].set(route_weight.reshape(-1).astype(jnp.float32), mode='drop').reshape(EXPERTS, SHARDS * CAP)
    positions = jnp.arange(TOKENS, dtype=jnp.int32) % TOK_DP
    cosine, sine_table = turn_tables(positions, QK_ROPE // 2)
    seq_cos = cosine[:TOK_DP]
    seq_sin = sine_table[:TOK_DP]
    scaling = (QK_NOPE + QK_ROPE) ** (-0.5)
    slice_width = FF_EXP // N_TENSOR
    seq_positions = jnp.arange(TOK_DP, dtype=jnp.int32)

    def forward(input_float, gain_mixer, weight_query, weight_latent, gain_latent, weight_up, weight_out, gain_experts, gate_experts, up_experts, down_experts, gate_common, up_common, down_common):
        normed_first = low(root_norm(input_float, gain_mixer))
        latent_all = low_back(jnp.dot(normed_first, weight_latent, precision=PRECISE))
        latent_norm = low(root_norm(latent_all[:, :KV_RANK], gain_latent))
        key_rope = low(rotate(latent_all[:, KV_RANK:], cosine, sine_table))

        def attend(pieces):
            normed_seq, latent_seq, rope_seq, doc_seq = pieces
            query_raw = low_back(jnp.dot(normed_seq, weight_query, precision=PRECISE)).reshape(TOK_DP, HEADS, QK_NOPE + QK_ROPE)
            query_cat = low(jnp.concatenate([query_raw[..., :QK_NOPE], rotate(query_raw[..., QK_NOPE:], seq_cos[:, None, :], seq_sin[:, None, :])], axis=-1))
            key_value = low(low_back(jnp.dot(latent_seq, weight_up, precision=PRECISE))).reshape(TOK_DP, HEADS, QK_NOPE + V_DIM)
            key_rows = jnp.concatenate([key_value[..., :QK_NOPE], jnp.broadcast_to(rope_seq[:, None, :], (TOK_DP, HEADS, QK_ROPE))], axis=-1)
            values = key_value[..., QK_NOPE:]
            scores = low_back(jnp.einsum('qhd,khd->hqk', query_cat, key_rows, precision=PRECISE) * scaling)
            allowed = (doc_seq[:, None] == doc_seq[None, :]) & (seq_positions[None, :] <= seq_positions[:, None])
            scores = jnp.where(allowed[None], scores, -1e+30)
            row_max = lax.optimization_barrier(jnp.max(scores, axis=-1, keepdims=True))
            exp_terms = jnp.exp(scores - row_max)
            prob_rows = exp_terms / lax.optimization_barrier(jnp.sum(exp_terms, axis=-1, keepdims=True))
            heads_out = jnp.einsum('hqk,khd->qhd', low(prob_rows), values, precision=PRECISE)
            heads_out = low(low_back(heads_out)).reshape(TOK_DP, HEADS * V_DIM)
            return jnp.dot(heads_out, weight_out, precision=PRECISE)
        mixer_out = lax.map(jax.checkpoint(attend), (normed_first.reshape(SEQS, TOK_DP, D), latent_norm.reshape(SEQS, TOK_DP, KV_RANK), key_rope.reshape(SEQS, TOK_DP, QK_ROPE), segment_ids)).reshape(TOKENS, D)
        hidden_state = input_float + low_back(mixer_out)
        normed_second = low(root_norm(hidden_state, gain_experts))
        gate_shared = low_back(jnp.dot(normed_second, gate_common, precision=PRECISE))
        up_shared = low_back(jnp.dot(normed_second, up_common, precision=PRECISE))
        hidden_shared = low(silu_of(gate_shared) * up_shared)
        shared_out = jnp.dot(hidden_shared, down_common, precision=PRECISE)

        def expert_step(routed_sum, pieces):
            weights_gate, weights_up, weights_down, tokens_here, weights_here = pieces
            rows_in = jnp.take(normed_second, tokens_here, axis=0, mode='fill', fill_value=0.0)
            copies = low_back(jnp.broadcast_to(rows_in[None], (N_TENSOR,) + rows_in.shape))
            gate_slices = jnp.transpose(weights_gate.reshape(D, N_TENSOR, slice_width), (1, 0, 2))
            up_slices = jnp.transpose(weights_up.reshape(D, N_TENSOR, slice_width), (1, 0, 2))
            down_slices = weights_down.reshape(N_TENSOR, slice_width, D)
            gate_val = low_back(jnp.einsum('srd,sdf->srf', copies, gate_slices, precision=PRECISE))
            up_val = low_back(jnp.einsum('srd,sdf->srf', copies, up_slices, precision=PRECISE))
            hidden_rows = low(silu_of(gate_val) * up_val)
            slice_out = low(jnp.einsum('srf,sfd->srd', hidden_rows, down_slices, precision=PRECISE))
            expert_out = low_back(lax.optimization_barrier(jnp.sum(slice_out, axis=0)))
            routed_sum = routed_sum.at[tokens_here].add(expert_out * weights_here[:, None], mode='drop')
            return (routed_sum, None)
        routed_sum, unused = lax.scan(jax.checkpoint(expert_step), jnp.zeros((TOKENS, D), jnp.float32), (gate_experts, up_experts, down_experts, slot_tokens, slot_weights))
        return hidden_state + routed_sum + shared_out
    primals = (layer_input.astype(jnp.float32), attention_gain.astype(jnp.float32), query_weight.astype(jnp.float32), latent_weight.astype(jnp.float32), latent_gain.astype(jnp.float32), latent_up.astype(jnp.float32), output_weight.astype(jnp.float32), experts_gain.astype(jnp.float32), expert_gate.astype(jnp.float32), expert_up.astype(jnp.float32), expert_down.astype(jnp.float32), shared_gate.astype(jnp.float32), shared_up.astype(jnp.float32), shared_down.astype(jnp.float32))
    result, pullback = jax.vjp(forward, *primals)
    gradients = pullback(out_cotangent.astype(jnp.float32))
    return (result.astype(jnp.bfloat16), gradients[0], gradients[1], gradients[2], gradients[3], gradients[4], gradients[5], gradients[6], gradients[7], gradients[8], gradients[9], gradients[10], gradients[11], gradients[12], gradients[13])
```

```python
import functools

import jax
import jax.numpy as jnp
from jax import lax
from jax.experimental import pallas as pl
from jax.experimental.pallas import tpu as pltpu
from jax.sharding import PartitionSpec as P

D = 2048
QK_NOPE = 128
QK_ROPE = 64
V_DIM = 128
KV_RANK = 512
TOPK = 6
NORM_EPS = 1e-06

BF = jnp.bfloat16
F32 = jnp.float32
BOTH = ("dp", "tensor")
CORE = 1
GB = 4
LANES = 128
VMEM_CAP = 60 * 1024 * 1024


def round_up(value, step):
    return (value + step - 1) // step * step


def root_norm(values, gain_row):
    factor = lax.rsqrt(jnp.mean(values * values, axis=-1, keepdims=True) + NORM_EPS)
    return values * factor * gain_row


def turn_tables(positions, half_width):
    frequency = 10000.0 ** (-jnp.arange(half_width, dtype=F32) / half_width)
    angles = positions.astype(F32)[:, None] * frequency[None, :]
    return (jnp.cos(angles), jnp.sin(angles))


def rotate(values, cosine, sine_table):
    half_width = values.shape[-1] // 2
    first_half = values[..., :half_width]
    second_half = values[..., half_width:]
    return jnp.concatenate(
        [
            first_half * cosine - second_half * sine_table,
            first_half * sine_table + second_half * cosine,
        ],
        axis=-1,
    )


def dot(left, right, dims=((1,), (0,))):
    return lax.dot_general(left, right, (dims, ((), ())), preferred_element_type=F32)


def swap_with(values, mask, count):
    return lax.ppermute(values, BOTH, [(i, i ^ mask) for i in range(count)])


def cube_gather(block, masks, count):
    for mask in masks:
        block = jnp.concatenate([block, swap_with(block, mask, count)], axis=0)
    return block


def tie(first, second):
    return lax.optimization_barrier((first, second))


def halve_stage(keeps, receiveds, masks, count):
    half = keeps[0].shape[0] // 2
    sent = [
        swap_with((k[half:].astype(F32) + r[half:].astype(F32)).astype(BF), mask, count)
        for k, r, mask in zip(keeps, receiveds, masks)
    ]
    lower = [k[:half].astype(F32) + r[:half].astype(F32) for k, r in zip(keeps, receiveds)]
    return lower, sent


def scatter_rows(partial, masks, count):
    for mask in masks:
        half = partial.shape[0] // 2
        received = swap_with(partial[half:].astype(BF), mask, count)
        partial = partial[:half].astype(F32) + received.astype(F32)
    return partial


def block_order(block, blocks, swapped):
    if not swapped:
        return block
    top, low = block // (blocks // 2), (block // (blocks // 4)) % 2
    return low * (blocks // 2) + top * (blocks // 4) + block % (blocks // 4)


def one_hot(slot_row, rows):
    tokens = lax.broadcasted_iota(jnp.int32, (rows, slot_row.shape[1]), 0)
    return jnp.where(tokens == slot_row, 1.0, 0.0).astype(BF)


def resident(shape):
    return pl.BlockSpec(shape, lambda *_: (0,) * len(shape), pipeline_mode=pl.Buffered(1))


def cotangent_rows(ids, slot_rows, slot_weights, cotangents, down_t, common_down_t):
    groups, _, slots = slot_rows.shape
    experts, _, width = down_t.shape
    cap = slots // experts
    rows = cotangents.shape[0] // groups
    units = common_down_t.shape[1]

    def body(ids_ref, slot_ref, weight_ref, g0, g1, g2, g3, down_ref, common_ref, rows_ref, dh_ref, dhs_ref):
        for k, g_ref in enumerate((g0, g1, g2, g3)):
            value = g_ref[...]
            picked = dot(one_hot(slot_ref[k], rows), value, ((0,), (0,))).astype(BF)
            for j in range(experts):
                rows_ref[j, k * cap : (k + 1) * cap, :] = picked[j * cap : (j + 1) * cap]
            dhs_ref[k * rows : (k + 1) * rows, :] = dot(value, common_ref[...])
        for j in range(experts):
            dh_ref[j] = dot(rows_ref[j], down_ref[j]) * weight_ref[j][:, :1]

    def row_block(k):
        return pl.BlockSpec((rows, D), lambda i, ids: (ids[GB * i + k], 0))

    return pl.pallas_call(
        body,
        grid_spec=pltpu.PrefetchScalarGridSpec(
            num_scalar_prefetch=1,
            grid=(groups // GB,),
            in_specs=[
                pl.BlockSpec((GB, 1, slots), lambda i, ids: (i, 0, 0)),
                pl.BlockSpec((experts, GB * cap, LANES), lambda i, ids: (0, i, 0)),
                *[row_block(k) for k in range(GB)],
                resident(down_t.shape),
                resident(common_down_t.shape),
            ],
            out_specs=[
                pl.BlockSpec((experts, GB * cap, D), lambda i, ids: (0, i, 0)),
                pl.BlockSpec((experts, GB * cap, width), lambda i, ids: (0, i, 0)),
                pl.BlockSpec((GB * rows, units), lambda i, ids: (i, 0)),
            ],
        ),
        out_shape=[
            jax.ShapeDtypeStruct((experts, groups * cap, D), BF),
            jax.ShapeDtypeStruct((experts, groups * cap, width), F32),
            jax.ShapeDtypeStruct((groups * rows, units), F32),
        ],
        compiler_params=pltpu.CompilerParams(vmem_limit_bytes=VMEM_CAP),
        name="cotangent_rows",
    )(ids, slot_rows, slot_weights, *([cotangents] * GB), down_t, common_down_t)


def expert_block(half, streams, order_flags, slot_rows, slot_weights, dh, dhs, weights, previous):
    gate_up, gate_up_t, common_t, common = weights
    groups, _, slots = slot_rows.shape
    experts, _, double = gate_up.shape
    width = double // 2
    cap = slots // experts
    blocks = groups // (2 * GB)
    rows = streams[0].shape[0] // (groups // 2)
    part = streams[0].shape[1]
    units = dhs.shape[1]
    count = len(streams)

    def body(*refs):
        slot_ref, weight_ref, dh_ref, dhs_ref = refs[:4]
        token_refs = refs[4 : 4 + count]
        gu_ref, gut_ref, common_t_ref, common_ref = refs[4 + count : 8 + count]
        x_ref, hidden_ref, dgu_ref, hs_ref, dgs_ref = refs[-(5 + count) : -count]
        out_refs = refs[-count:]
        for k in range(GB):
            picks = one_hot(slot_ref[k], rows)
            for s in range(count):
                picked = dot(
                    picks, token_refs[s][k * rows : (k + 1) * rows, :], ((0,), (0,))
                ).astype(BF)
                for j in range(experts):
                    x_ref[j, k * cap : (k + 1) * cap, s * part : (s + 1) * part] = picked[
                        j * cap : (j + 1) * cap
                    ]
        common_gu = dot(token_refs[0][...], common_t_ref[:part, :])
        for s in range(1, count):
            common_gu += dot(token_refs[s][...], common_t_ref[s * part : (s + 1) * part, :])
        gate, up = common_gu[:, :units], common_gu[:, units:]
        logistic = jax.nn.sigmoid(gate)
        silu = gate * logistic
        hs_ref[...] = (silu * up).astype(BF)
        grad_hidden = dhs_ref[...]
        slope = logistic * (1.0 + gate * (1.0 - logistic))
        dgs_ref[:, :units] = (grad_hidden * up * slope).astype(BF)
        dgs_ref[:, units:] = (grad_hidden * silu).astype(BF)
        grads = []
        for j in range(experts):
            both = dot(x_ref[j], gu_ref[j])
            gate, up = both[:, :width], both[:, width:]
            logistic = jax.nn.sigmoid(gate)
            silu = gate * logistic
            hidden_ref[j] = (silu * up * weight_ref[j][:, :1]).astype(BF)
            grad_hidden = dh_ref[j]
            slope = logistic * (1.0 + gate * (1.0 - logistic))
            dgu_ref[j, :, :width] = (grad_hidden * up * slope).astype(BF)
            dgu_ref[j, :, width:] = (grad_hidden * silu).astype(BF)
            grads.append(dot(dgu_ref[j], gut_ref[j]).astype(BF))
        for k in range(GB):
            picks = one_hot(slot_ref[k], rows)
            stacked = jnp.concatenate([g[k * cap : (k + 1) * cap] for g in grads], axis=0)
            total = dot(picks, stacked) + dot(
                dgs_ref[k * rows : (k + 1) * rows, :], common_ref[...]
            )
            for s in range(count):
                out_refs[s][k * rows : (k + 1) * rows, :] = total[
                    :, s * part : (s + 1) * part
                ].astype(BF)

    shift = half * blocks
    token_specs = [
        pl.BlockSpec((GB * rows, part), functools.partial(lambda f, i: (block_order(i, blocks, f), 0), flag))
        for flag in order_flags
    ]
    in_specs = [
        pl.BlockSpec((GB, 1, slots), lambda i: (shift + i, 0, 0)),
        pl.BlockSpec((experts, GB * cap, LANES), lambda i: (0, shift + i, 0)),
        pl.BlockSpec((experts, GB * cap, width), lambda i: (0, shift + i, 0)),
        pl.BlockSpec((GB * rows, units), lambda i: (shift + i, 0)),
        *token_specs,
        resident(gate_up.shape),
        resident(gate_up_t.shape),
        resident(common_t.shape),
        resident(common.shape),
    ]
    operands = [slot_rows, slot_weights, dh, dhs, *streams, gate_up, gate_up_t, common_t, common]
    aliases = {}
    if previous is not None:
        for at, value in enumerate(previous):
            aliases[len(operands)] = at
            in_specs.append(pl.BlockSpec(memory_space=pl.ANY))
            operands.append(value)
    outs = pl.pallas_call(
        body,
        grid=(blocks,),
        in_specs=in_specs,
        out_specs=[
            pl.BlockSpec((experts, GB * cap, D), lambda i: (0, shift + i, 0)),
            pl.BlockSpec((experts, GB * cap, width), lambda i: (0, shift + i, 0)),
            pl.BlockSpec((experts, GB * cap, double), lambda i: (0, shift + i, 0)),
            pl.BlockSpec((GB * rows, units), lambda i: (shift + i, 0)),
            pl.BlockSpec((GB * rows, 2 * units), lambda i: (shift + i, 0)),
            *token_specs,
        ],
        out_shape=[
            jax.ShapeDtypeStruct((experts, groups * cap, D), BF),
            jax.ShapeDtypeStruct((experts, groups * cap, width), BF),
            jax.ShapeDtypeStruct((experts, groups * cap, double), BF),
            jax.ShapeDtypeStruct((groups * rows, units), BF),
            jax.ShapeDtypeStruct((groups * rows, 2 * units), BF),
            *[jax.ShapeDtypeStruct(s.shape, BF) for s in streams],
        ],
        input_output_aliases=aliases,
        compiler_params=pltpu.CompilerParams(vmem_limit_bytes=VMEM_CAP),
        name="expert_block",
    )(*operands)
    return outs[:5], outs[5:]


def combine_rows(ids, slot_rows, expert_rows, hidden_common, common_down):
    groups, _, slots = slot_rows.shape
    experts = len(expert_rows)
    cap = slots // experts
    rows = hidden_common.shape[0] // groups

    def body(ids_ref, slot_ref, *refs):
        row_refs = refs[:experts]
        hs_ref, down_ref, out_ref = refs[experts:]
        stacked = jnp.concatenate([r[...] for r in row_refs], axis=0)
        total = dot(one_hot(slot_ref[0], rows), stacked) + dot(hs_ref[...], down_ref[...])
        out_ref[...] = total.astype(BF)

    return pl.pallas_call(
        body,
        grid_spec=pltpu.PrefetchScalarGridSpec(
            num_scalar_prefetch=1,
            grid=(groups,),
            in_specs=[
                pl.BlockSpec((1, 1, slots), lambda i, ids: (i, 0, 0)),
                *[pl.BlockSpec((cap, D), lambda i, ids: (i, 0)) for _ in range(experts)],
                pl.BlockSpec((rows, hidden_common.shape[1]), lambda i, ids: (i, 0)),
                resident(common_down.shape),
            ],
            out_specs=pl.BlockSpec((rows, D), lambda i, ids: (ids[i], 0)),
        ),
        out_shape=jax.ShapeDtypeStruct((groups * rows, D), BF),
        compiler_params=pltpu.CompilerParams(vmem_limit_bytes=VMEM_CAP),
        name="combine_rows",
    )(ids, slot_rows, *expert_rows, hidden_common, common_down)


def slot_tables(routes, route_weight, place_order, expert_total, capacity, padded):
    shard_rows = routes.shape[0]
    pair_count = shard_rows * TOPK
    expert_ids = routes.reshape(pair_count)
    ranks = place_order[0]
    earlier = (expert_ids[:, None] == expert_ids[None, :]) & (ranks[None, :] < ranks[:, None])
    places = jnp.sum(earlier.astype(jnp.int32), axis=1)
    slots = jnp.where(places < capacity, expert_ids * padded + places, -1)
    chosen = slots[:, None] == jnp.arange(expert_total * padded, dtype=jnp.int32)[None, :]
    pair_tokens = (jnp.arange(pair_count, dtype=jnp.int32) // TOPK).astype(F32)
    tokens = shard_rows + jnp.sum(
        jnp.where(chosen, pair_tokens[:, None] - shard_rows, 0.0), axis=0
    )
    weights = jnp.sum(jnp.where(chosen, route_weight.reshape(pair_count)[:, None], 0.0), axis=0)
    return jnp.stack([tokens, weights])


def norm_back(values, gain_row, grads):
    factor = lax.rsqrt(jnp.mean(values * values, axis=-1, keepdims=True) + NORM_EPS)
    scaled = gain_row * grads
    inner = jnp.mean(values * scaled, axis=-1, keepdims=True)
    grad_values = factor * scaled - values * (factor * factor * factor) * inner
    grad_gain = jnp.sum(grads * values * factor, axis=0)
    return grad_values, grad_gain


def local(
    layer_input,
    segment_ids,
    routes,
    route_weight,
    place_order,
    attention_gain,
    query_weight,
    latent_weight,
    latent_gain,
    latent_up,
    output_weight,
    experts_gain,
    expert_gate,
    expert_up,
    expert_down,
    shared_gate,
    shared_up,
    shared_down,
    out_cotangent,
):
    tensor_count = lax.axis_size("tensor")
    dp_count = lax.axis_size("dp")
    count = tensor_count * dp_count
    dp_at = lax.axis_index("dp")
    tensor_at = lax.axis_index("tensor")
    me = dp_at * tensor_count + tensor_at
    shard_rows = layer_input.shape[0]
    seq_len = segment_ids.shape[1]
    row_block = D // dp_count
    outer = [1 << b for b in range(count.bit_length() - 2, 0, -1)]
    order_a = tuple(outer)
    order_b = tuple(outer[:-2] + [outer[-1], outer[-2]])
    stream_orders = (order_a, order_b, order_a, order_b)
    order_flags = (False, True, False, True)
    part = D // len(stream_orders)
    tensor_masks = tuple(1 << b for b in range(tensor_count.bit_length() - 2, -1, -1))

    up_split = row_block // latent_up.shape[0]
    latent_pad = round_up(KV_RANK + QK_ROPE + 3, LANES)
    extras = jnp.concatenate(
        [
            latent_weight,
            attention_gain[:, None],
            experts_gain[:, None],
            jnp.broadcast_to(latent_gain[:, None], (latent_gain.shape[0], up_split)).reshape(-1, 1),
            jnp.zeros((row_block, latent_pad - KV_RANK - QK_ROPE - 3), BF),
        ],
        axis=1,
    )
    query_cols = query_weight.shape[1]
    out_cols = output_weight.shape[0]
    up_cols = latent_up.shape[1] // up_split
    packed = jnp.concatenate(
        [query_weight, output_weight.T, latent_up.reshape(row_block, up_cols), extras], axis=1
    )
    packed_full = lax.all_gather(packed, "dp", axis=0, tiled=True)
    hidden_total = shared_gate.shape[1]
    unit_block = hidden_total // tensor_count
    units = unit_block // dp_count
    unit_pad = round_up(units, LANES)
    column = tensor_at * unit_block
    common_send = jnp.stack(
        [
            lax.dynamic_slice_in_dim(shared_gate, column, unit_block, 1).T,
            lax.dynamic_slice_in_dim(shared_up, column, unit_block, 1).T,
            lax.dynamic_slice_in_dim(shared_down, column, unit_block, 0),
        ]
    ).reshape(3, dp_count, units, row_block)
    common_here = lax.all_to_all(
        jnp.transpose(common_send, (1, 0, 2, 3)), "dp", split_axis=0, concat_axis=0, tiled=True
    )
    common_here = jnp.transpose(common_here, (1, 2, 0, 3)).reshape(3, units, D)
    common_here = jnp.pad(common_here, ((0, 0), (0, unit_pad - units), (0, 0)))
    common_gu = common_here[:2].reshape(2 * unit_pad, D)
    common_down = common_here[2]
    common_gu_t = common_gu.T
    common_down_t = common_down.T

    expert_local = expert_gate.shape[0]
    expert_total = expert_local * dp_count
    capacity = max(2, 5 * shard_rows * TOPK // (4 * expert_total))
    padded = round_up(capacity, 16)
    slots = expert_local * padded
    tables = slot_tables(routes, route_weight, place_order, expert_total, capacity, padded)
    tables_all = cube_gather(tables[None], order_a + (CORE,), count)
    tables_mine = lax.dynamic_slice_in_dim(tables_all, dp_at * slots, slots, 2)
    relative = jnp.zeros((count,), jnp.int32)
    canon = jnp.arange(count, dtype=jnp.int32)
    for bit, mask in enumerate(order_a + (CORE,)):
        relative = relative + mask * ((canon >> bit) & 1)
    group_ids = me ^ relative
    slot_rows = tables_mine[:, :1, :].astype(jnp.int32)
    slot_weights = jnp.transpose(
        tables_mine[:, 1, :].reshape(count, expert_local, padded), (1, 0, 2)
    ).reshape(expert_local, count * padded, 1)
    slot_weights = jnp.broadcast_to(slot_weights, (expert_local, count * padded, LANES))

    width = expert_gate.shape[2]
    width_pad = round_up(width, LANES)
    pad_columns = ((0, 0), (0, 0), (0, width_pad - width))
    gate_up = jnp.concatenate(
        [jnp.pad(expert_gate, pad_columns), jnp.pad(expert_up, pad_columns)], axis=2
    )
    gate_up_t = jnp.transpose(gate_up, (0, 2, 1))
    down_pad = jnp.pad(expert_down, ((0, 0), (0, width_pad - width), (0, 0)))
    down_t = jnp.transpose(down_pad, (0, 2, 1))

    input_seq = cube_gather(layer_input, tensor_masks, count)
    ready = (gate_up, gate_up_t, down_pad, down_t, common_gu, common_gu_t, common_down, common_down_t)
    packed_full, (ready, slot_rows, slot_weights, input_seq) = tie(
        packed_full, (ready, slot_rows, slot_weights, input_seq)
    )
    gate_up, gate_up_t, down_pad, down_t, common_gu, common_gu_t, common_down, common_down_t = ready
    at = query_cols
    weight_query = packed_full[:, :at]
    weight_out_t = packed_full[:, at : at + out_cols]
    at += out_cols
    weight_up = packed_full[:, at : at + up_cols].reshape(KV_RANK, up_split * up_cols)
    at += up_cols
    weight_latent = packed_full[:, at : at + KV_RANK + QK_ROPE]
    at += KV_RANK + QK_ROPE
    mixer_scale = packed_full[:, at].astype(F32)
    experts_scale = packed_full[:, at + 1].astype(F32)
    latent_scale = packed_full[:, at + 2].reshape(KV_RANK, up_split)[:, 0].astype(F32)

    input_float = layer_input.astype(F32)
    hops = jnp.zeros((tensor_count,), jnp.int32)
    seq_blocks = jnp.arange(tensor_count, dtype=jnp.int32)
    for bit, mask in enumerate(tensor_masks):
        hops = hops + mask * ((seq_blocks >> bit) & 1)
    block_ids = tensor_at ^ hops
    positions = (
        block_ids[:, None] * shard_rows + jnp.arange(shard_rows, dtype=jnp.int32)[None, :]
    ).reshape(seq_len)
    doc_ids = jnp.take(segment_ids[0].reshape(tensor_count, shard_rows), block_ids, axis=0)
    doc_ids = doc_ids.reshape(seq_len)
    seq_cos, seq_sin = turn_tables(positions, QK_ROPE // 2)
    normed_full = root_norm(input_seq.astype(F32), mixer_scale).astype(BF)
    normed_first = normed_full[:shard_rows]
    latent_all = dot(normed_full, weight_latent)
    latent_full = root_norm(latent_all[:, :KV_RANK], latent_scale).astype(BF)
    rope_full = rotate(latent_all[:, KV_RANK:], seq_cos, seq_sin).astype(BF)
    latent_raw = latent_all[:shard_rows, :KV_RANK]
    head_dim = QK_NOPE + QK_ROPE
    local_heads = query_cols // head_dim
    query_raw = dot(normed_full, weight_query).reshape(seq_len, local_heads, head_dim)
    query_cat = jnp.concatenate(
        [
            query_raw[..., :QK_NOPE],
            rotate(query_raw[..., QK_NOPE:], seq_cos[:, None, :], seq_sin[:, None, :]),
        ],
        axis=-1,
    ).astype(BF)
    key_value = dot(latent_full, weight_up).astype(BF)
    key_value = key_value.reshape(seq_len, local_heads, QK_NOPE + V_DIM)
    key_rows = jnp.concatenate(
        [
            key_value[..., :QK_NOPE],
            jnp.broadcast_to(rope_full[:, None, :], (seq_len, local_heads, QK_ROPE)),
        ],
        axis=-1,
    )
    values = key_value[..., QK_NOPE:]
    scaling = head_dim ** (-0.5)
    raw_scores = jnp.einsum("qhd,khd->hqk", query_cat, key_rows, preferred_element_type=F32)
    raw_scores = raw_scores * scaling
    allowed = (doc_ids[:, None] == doc_ids[None, :]) & (positions[None, :] <= positions[:, None])
    masked = jnp.where(allowed[None], raw_scores, -1e30)
    row_max = jnp.max(masked, axis=-1, keepdims=True)
    exp_terms = jnp.exp(masked - row_max)
    row_total = jnp.sum(exp_terms, axis=-1, keepdims=True)
    prob_rows = exp_terms / row_total
    heads_out = jnp.einsum("hqk,khd->qhd", prob_rows.astype(BF), values, preferred_element_type=F32)
    heads_out = heads_out.astype(BF).reshape(seq_len, local_heads * V_DIM)
    mixer_terms = dot(heads_out, weight_out_t, ((1,), (1,)))
    mixer_out = scatter_rows(mixer_terms, tensor_masks[::-1], count)
    hidden_state = input_float + mixer_out
    normed_second = root_norm(hidden_state, experts_scale).astype(BF)

    cotangent_all = lax.all_gather(out_cotangent, BOTH, axis=0, tiled=True)
    grad_rows, grad_hidden, grad_hidden_common = cotangent_rows(
        group_ids, slot_rows, slot_weights, cotangent_all, down_t, common_down_t
    )

    near = [
        cube_gather(normed_second[:, s * part : (s + 1) * part], order[:-1], count)
        for s, order in enumerate(stream_orders)
    ]
    last = [swap_with(block, order[-1], count) for block, order in zip(near, stream_orders)]
    last, (grad_rows, grad_hidden, grad_hidden_common) = tie(
        last, (grad_rows, grad_hidden, grad_hidden_common)
    )
    near = [jnp.concatenate(pair, axis=0) for pair in zip(near, last)]
    far = [swap_with(block, CORE, count) for block in near]
    expert_weights = (gate_up, gate_up_t, common_gu_t, common_gu)
    kept, far_terms = expert_block(
        1, far, order_flags, slot_rows, slot_weights, grad_hidden, grad_hidden_common,
        expert_weights, None,
    )
    far_received = [swap_with(term, CORE, count) for term in far_terms]
    kept, near_terms = expert_block(
        0, near, order_flags, slot_rows, slot_weights, grad_hidden, grad_hidden_common,
        expert_weights, kept,
    )
    rows_in, hidden_rows, grad_gu, hidden_common, grad_common = kept
    half_rows = count // 2 * shard_rows
    parts = []
    for s, flag in enumerate(order_flags):
        total = 0.0
        for h, tokens in ((0, near[s]), (1, far[s])):
            grads = grad_common[h * half_rows : (h + 1) * half_rows]
            if flag:
                shape = (2, 2, half_rows // 4, 2 * unit_pad)
                grads = jnp.swapaxes(grads.reshape(shape), 0, 1).reshape(half_rows, 2 * unit_pad)
            total = total + dot(grads, tokens, ((0,), (0,)))
        parts.append(total)
    grad_common_gu = jnp.concatenate(parts, axis=1)
    if count > 32:
        near_terms, grad_common_gu = tie(near_terms, grad_common_gu)
    turns = [order[::-1] for order in stream_orders]

    lower, sent = halve_stage(near_terms, far_received, [turn[0] for turn in turns], count)
    expert_rows = [dot(hidden_rows[j], down_pad[j]).astype(BF) for j in range(expert_local)]
    result_terms = combine_rows(group_ids, slot_rows, expert_rows, hidden_common, common_down)
    sent, result_terms = tie(sent, result_terms)

    lower, sent = halve_stage(lower, sent, [turn[1] for turn in turns], count)
    grad_expert_gate = jnp.stack(
        [dot(rows_in[j], grad_gu[j, :, :width], ((0,), (0,))) for j in range(expert_local)]
    )
    sent, grad_expert_gate = tie(sent, grad_expert_gate)
    lower, sent = halve_stage(lower, sent, [turn[2] for turn in turns], count)
    grad_expert_up = jnp.stack(
        [
            dot(rows_in[j], grad_gu[j, :, width_pad : width_pad + width], ((0,), (0,)))
            for j in range(expert_local)
        ]
    )
    sent, grad_expert_up = tie(sent, grad_expert_up)
    for k in range(3, len(order_a)):
        lower, sent = halve_stage(lower, sent, [turn[k] for turn in turns], count)
    grad_normed_second = jnp.concatenate(
        [a + b.astype(F32) for a, b in zip(lower, sent)], axis=1
    )
    grad_expert_down = jnp.stack(
        [dot(hidden_rows[j][:, :width], grad_rows[j], ((0,), (0,))) for j in range(expert_local)]
    )

    canon_ids = jnp.zeros((count,), jnp.int32)
    offset = me ^ canon
    for bit, mask in enumerate(order_a + (CORE,)):
        canon_ids = canon_ids + (1 << bit) * ((offset // mask) & 1)
    hidden_global = jnp.take(
        hidden_common.reshape(count, shard_rows, unit_pad), canon_ids, axis=0
    ).reshape(count * shard_rows, unit_pad)
    if count > 32:
        again, _ = tie(out_cotangent, grad_normed_second)
        cotangent_all = lax.all_gather(again, BOTH, axis=0, tiled=True)
    grad_common_down = dot(hidden_global, cotangent_all, ((0,), (0,)))
    common_grads = jnp.stack(
        [grad_common_gu[:units], grad_common_gu[unit_pad : unit_pad + units], grad_common_down[:units]]
    ).astype(BF)
    common_grads = jnp.transpose(
        common_grads.reshape(3, units, dp_count, row_block), (2, 0, 1, 3)
    )
    common_grads = lax.all_to_all(common_grads, "dp", split_axis=0, concat_axis=0, tiled=True)
    common_grads = jnp.transpose(common_grads, (1, 0, 2, 3)).reshape(3, unit_block, row_block)
    grad_shared_gate = common_grads[0].T.astype(F32)
    grad_shared_up = common_grads[1].T.astype(F32)
    grad_shared_down = common_grads[2].astype(F32)

    if count > 32:
        result_terms, _ = tie(
            result_terms, (grad_normed_second, common_grads, grad_expert_down)
        )
    result = lax.psum_scatter(result_terms, BOTH, scatter_dimension=0, tiled=True)
    cotangent = out_cotangent.astype(F32)
    grad_from_experts, grad_experts_part = norm_back(hidden_state, experts_scale, grad_normed_second)
    grad_hidden_state = cotangent + grad_from_experts
    grad_mixer_full = cube_gather(grad_hidden_state.astype(BF), tensor_masks, count)
    grad_output_t = dot(grad_mixer_full, heads_out, ((0,), (0,)))
    grad_heads = dot(grad_mixer_full, weight_out_t).astype(BF)
    grad_heads = grad_heads.reshape(seq_len, local_heads, V_DIM)
    grad_probs = jnp.einsum("qhd,khd->hqk", grad_heads, values, preferred_element_type=F32)
    row_dot = jnp.sum(prob_rows * grad_probs, axis=-1, keepdims=True)
    grad_scores = (prob_rows * (grad_probs - row_dot)).astype(BF)
    grad_query = scaling * jnp.einsum(
        "hqk,khd->qhd", grad_scores, key_rows, preferred_element_type=F32
    )
    grad_keys = scaling * jnp.einsum(
        "hqk,qhd->khd", grad_scores, query_cat, preferred_element_type=F32
    )
    grad_values = jnp.einsum(
        "hqk,qhd->khd", prob_rows.astype(BF), grad_heads, preferred_element_type=F32
    )
    grad_query_raw = (
        jnp.concatenate(
            [
                grad_query[..., :QK_NOPE],
                rotate(grad_query[..., QK_NOPE:], seq_cos[:, None, :], -seq_sin[:, None, :]),
            ],
            axis=-1,
        )
        .reshape(seq_len, local_heads * head_dim)
        .astype(BF)
    )
    grad_key_value = (
        jnp.concatenate([grad_keys[..., :QK_NOPE], grad_values], axis=-1)
        .reshape(seq_len, local_heads * (QK_NOPE + V_DIM))
        .astype(BF)
    )
    grad_terms = jnp.concatenate(
        [
            dot(grad_query_raw, weight_query, ((1,), (1,))).astype(BF),
            dot(grad_key_value, weight_up, ((1,), (1,))).astype(BF),
            jnp.sum(grad_keys[..., QK_NOPE:], axis=1).astype(BF),
            jnp.zeros((seq_len, QK_ROPE), BF),
        ],
        axis=1,
    )
    grad_shard = scatter_rows(grad_terms, tensor_masks[::-1], count)
    grad_query_local = dot(normed_full, grad_query_raw, ((0,), (0,)))
    grad_up_local = dot(latent_full, grad_key_value, ((0,), (0,)))
    weight_terms = jnp.concatenate(
        [
            grad_query_local.astype(BF),
            grad_output_t.astype(BF),
            grad_up_local.astype(BF).reshape(D, up_cols),
        ],
        axis=1,
    )
    weight_grads = lax.psum_scatter(weight_terms, "dp", scatter_dimension=0, tiled=True)
    weight_grads = weight_grads.astype(F32)
    grad_query_weight = weight_grads[:, :query_cols]
    grad_output_weight = weight_grads[:, query_cols : query_cols + out_cols].T
    grad_latent_up = weight_grads[:, query_cols + out_cols :].reshape(latent_up.shape)

    grad_latent_raw, grad_latent_part = norm_back(
        latent_raw, latent_scale, grad_shard[:, D : D + KV_RANK]
    )
    grad_rope = rotate(
        grad_shard[:, D + KV_RANK : D + KV_RANK + QK_ROPE],
        seq_cos[:shard_rows],
        -seq_sin[:shard_rows],
    )
    grad_latent_all = jnp.concatenate([grad_latent_raw, grad_rope], axis=-1).astype(BF)
    grad_latent_local = dot(normed_first, grad_latent_all, ((0,), (0,)))
    grad_normed_first = grad_shard[:, :D] + dot(grad_latent_all, weight_latent, ((1,), (1,)))
    grad_from_mixer, grad_mixer_part = norm_back(input_float, mixer_scale, grad_normed_first)
    grad_input = grad_hidden_state + grad_from_mixer
    gain_rows = D // KV_RANK
    latent_part = jnp.pad(
        grad_latent_part.reshape(count, KV_RANK // count),
        ((0, 0), (0, (gain_rows - 1) * KV_RANK // count)),
    ).reshape(D, 1)
    small_terms = jnp.concatenate(
        [
            grad_latent_local,
            grad_mixer_part[:, None],
            grad_experts_part[:, None],
            latent_part,
            jnp.zeros((D, latent_pad - KV_RANK - QK_ROPE - 3), F32),
        ],
        axis=1,
    ).astype(BF)
    small_terms = jnp.take(small_terms.reshape(count, D // count, latent_pad), group_ids, axis=0)
    small_grads = scatter_rows(
        small_terms.reshape(D, latent_pad), (CORE,) + order_a[::-1], count
    )
    at = KV_RANK + QK_ROPE
    grad_latent_weight = small_grads[:, :at]
    grad_attention_gain = small_grads[:, at]
    grad_experts_gain = small_grads[:, at + 1]
    grad_latent_gain = small_grads[: KV_RANK // count, at + 2]
    result, grad_input = tie(result, grad_input)
    layer_output = (hidden_state + result.astype(F32)).astype(BF)
    return (
        layer_output,
        grad_input,
        grad_attention_gain,
        grad_query_weight,
        grad_latent_weight,
        grad_latent_gain,
        grad_latent_up,
        grad_output_weight,
        grad_experts_gain,
        grad_expert_gate,
        grad_expert_up,
        grad_expert_down,
        grad_shared_gate,
        grad_shared_up,
        grad_shared_down,
    )


def solution(mesh):
    return jax.shard_map(
        local,
        mesh=mesh,
        in_specs=(
            P(("dp", "tensor"), None),
            P("dp", None),
            P(("dp", "tensor"), None),
            P(("dp", "tensor"), None),
            P(("dp", "tensor"), None),
            P("dp"),
            P("dp", "tensor"),
            P("dp", None),
            P("dp"),
            P("dp", "tensor"),
            P("tensor", "dp"),
            P("dp"),
            P("dp", None, "tensor"),
            P("dp", None, "tensor"),
            P("dp", "tensor", None),
            P("dp", None),
            P("dp", None),
            P(None, "dp"),
            P(("dp", "tensor"), None),
        ),
        out_specs=(
            P(("dp", "tensor"), None),
            P(("dp", "tensor"), None),
            P(("dp", "tensor")),
            P("dp", "tensor"),
            P(("dp", "tensor"), None),
            P(("dp", "tensor")),
            P("dp", "tensor"),
            P("tensor", "dp"),
            P(("dp", "tensor")),
            P("dp", None, "tensor"),
            P("dp", None, "tensor"),
            P("dp", "tensor", None),
            P("dp", "tensor"),
            P("dp", "tensor"),
            P("tensor", "dp"),
        ),
        check_vma=False,
    )
```

```python
import functools

import jax
import jax.numpy as jnp
from jax import lax
from jax.experimental import pallas as pl
from jax.experimental.pallas import tpu as pltpu
from jax.sharding import PartitionSpec as P

D = 2048
QK_NOPE = 128
QK_ROPE = 64
V_DIM = 128
KV_RANK = 512
TOPK = 6
NORM_EPS = 1e-06

BF = jnp.bfloat16
F32 = jnp.float32
BOTH = ("dp", "tensor")
CORE = 1
GB = 4
LANES = 128
VMEM_CAP = 60 * 1024 * 1024


def round_up(value, step):
    return (value + step - 1) // step * step


def root_norm(values, gain_row):
    factor = lax.rsqrt(jnp.mean(values * values, axis=-1, keepdims=True) + NORM_EPS)
    return values * factor * gain_row


def turn_tables(positions, half_width):
    frequency = 10000.0 ** (-jnp.arange(half_width, dtype=F32) / half_width)
    angles = positions.astype(F32)[:, None] * frequency[None, :]
    return (jnp.cos(angles), jnp.sin(angles))


def rotate(values, cosine, sine_table):
    half_width = values.shape[-1] // 2
    first_half = values[..., :half_width]
    second_half = values[..., half_width:]
    return jnp.concatenate(
        [
            first_half * cosine - second_half * sine_table,
            first_half * sine_table + second_half * cosine,
        ],
        axis=-1,
    )


def dot(left, right, dims=((1,), (0,))):
    return lax.dot_general(left, right, (dims, ((), ())), preferred_element_type=F32)


def swap_with(values, mask, count):
    return lax.ppermute(values, BOTH, [(i, i ^ mask) for i in range(count)])


def cube_gather(block, masks, count):
    for mask in masks:
        block = jnp.concatenate([block, swap_with(block, mask, count)], axis=0)
    return block


def tie(first, second):
    return lax.optimization_barrier((first, second))


def halve_stage(keeps, receiveds, masks, count, follow=()):
    half = keeps[0].shape[0] // 2
    upper = [
        (k[half:].astype(F32) + r[half:].astype(F32)).astype(BF)
        for k, r in zip(keeps, receiveds)
    ]
    upper, follow = tie(upper, follow)
    sent = [swap_with(value, mask, count) for value, mask in zip(upper, masks)]
    lower = [k[:half].astype(F32) + r[:half].astype(F32) for k, r in zip(keeps, receiveds)]
    return lower, sent, follow


def scatter_rows(partial, masks, count):
    for mask in masks:
        half = partial.shape[0] // 2
        received = swap_with(partial[half:].astype(BF), mask, count)
        partial = partial[:half].astype(F32) + received.astype(F32)
    return partial


def block_order(block, blocks, swapped):
    if not swapped:
        return block
    top, low = block // (blocks // 2), (block // (blocks // 4)) % 2
    return low * (blocks // 2) + top * (blocks // 4) + block % (blocks // 4)


def one_hot(slot_row, rows):
    tokens = lax.broadcasted_iota(jnp.int32, (rows, slot_row.shape[1]), 0)
    return jnp.where(tokens == slot_row, 1.0, 0.0).astype(BF)


def resident(shape):
    return pl.BlockSpec(shape, lambda *_: (0,) * len(shape), pipeline_mode=pl.Buffered(1))


def cotangent_rows(ids, slot_rows, slot_weights, cotangents, down_t, common_down_t):
    groups, _, slots = slot_rows.shape
    experts, _, width = down_t.shape
    cap = slots // experts
    rows = cotangents.shape[0] // groups
    units = common_down_t.shape[1]

    def body(ids_ref, slot_ref, weight_ref, g0, g1, g2, g3, down_ref, common_ref, rows_ref, dh_ref, dhs_ref):
        for k, g_ref in enumerate((g0, g1, g2, g3)):
            value = g_ref[...]
            picked = dot(one_hot(slot_ref[k], rows), value, ((0,), (0,))).astype(BF)
            for j in range(experts):
                rows_ref[j, k * cap : (k + 1) * cap, :] = picked[j * cap : (j + 1) * cap]
            dhs_ref[k * rows : (k + 1) * rows, :] = dot(value, common_ref[...])
        for j in range(experts):
            dh_ref[j] = dot(rows_ref[j], down_ref[j]) * weight_ref[j][:, :1]

    def row_block(k):
        return pl.BlockSpec((rows, D), lambda i, ids: (ids[GB * i + k], 0))

    return pl.pallas_call(
        body,
        grid_spec=pltpu.PrefetchScalarGridSpec(
            num_scalar_prefetch=1,
            grid=(groups // GB,),
            in_specs=[
                pl.BlockSpec((GB, 1, slots), lambda i, ids: (i, 0, 0)),
                pl.BlockSpec((experts, GB * cap, LANES), lambda i, ids: (0, i, 0)),
                *[row_block(k) for k in range(GB)],
                resident(down_t.shape),
                resident(common_down_t.shape),
            ],
            out_specs=[
                pl.BlockSpec((experts, GB * cap, D), lambda i, ids: (0, i, 0)),
                pl.BlockSpec((experts, GB * cap, width), lambda i, ids: (0, i, 0)),
                pl.BlockSpec((GB * rows, units), lambda i, ids: (i, 0)),
            ],
        ),
        out_shape=[
            jax.ShapeDtypeStruct((experts, groups * cap, D), BF),
            jax.ShapeDtypeStruct((experts, groups * cap, width), F32),
            jax.ShapeDtypeStruct((groups * rows, units), F32),
        ],
        compiler_params=pltpu.CompilerParams(vmem_limit_bytes=VMEM_CAP),
        name="cotangent_rows",
    )(ids, slot_rows, slot_weights, *([cotangents] * GB), down_t, common_down_t)


def expert_hidden(half, streams, order_flags, slot_rows, slot_weights, dh, dhs, weights, previous):
    gate_up, common_t = weights
    groups, _, slots = slot_rows.shape
    experts, _, double = gate_up.shape
    width = double // 2
    cap = slots // experts
    blocks = groups // (2 * GB)
    rows = streams[0].shape[0] // (groups // 2)
    part = streams[0].shape[1]
    units = dhs.shape[1]
    count = len(streams)

    def body(*refs):
        slot_ref, weight_ref, dh_ref, dhs_ref = refs[:4]
        token_refs = refs[4 : 4 + count]
        gu_ref, common_t_ref = refs[4 + count : 6 + count]
        x_ref, hidden_ref, dgu_ref, hs_ref, dgs_ref = refs[-5:]
        for k in range(GB):
            picks = one_hot(slot_ref[k], rows)
            for s in range(count):
                picked = dot(
                    picks, token_refs[s][k * rows : (k + 1) * rows, :], ((0,), (0,))
                ).astype(BF)
                for j in range(experts):
                    x_ref[j, k * cap : (k + 1) * cap, s * part : (s + 1) * part] = picked[
                        j * cap : (j + 1) * cap
                    ]
        common_gu = dot(token_refs[0][...], common_t_ref[:part, :])
        for s in range(1, count):
            common_gu += dot(token_refs[s][...], common_t_ref[s * part : (s + 1) * part, :])
        gate, up = common_gu[:, :units], common_gu[:, units:]
        logistic = jax.nn.sigmoid(gate)
        silu = gate * logistic
        hs_ref[...] = (silu * up).astype(BF)
        grad_hidden = dhs_ref[...]
        slope = logistic * (1.0 + gate * (1.0 - logistic))
        dgs_ref[:, :units] = (grad_hidden * up * slope).astype(BF)
        dgs_ref[:, units:] = (grad_hidden * silu).astype(BF)
        for j in range(experts):
            both = dot(x_ref[j], gu_ref[j])
            gate, up = both[:, :width], both[:, width:]
            logistic = jax.nn.sigmoid(gate)
            silu = gate * logistic
            hidden_ref[j] = (silu * up * weight_ref[j][:, :1]).astype(BF)
            grad_hidden = dh_ref[j]
            slope = logistic * (1.0 + gate * (1.0 - logistic))
            dgu_ref[j, :, :width] = (grad_hidden * up * slope).astype(BF)
            dgu_ref[j, :, width:] = (grad_hidden * silu).astype(BF)

    shift = half * blocks
    token_specs = [
        pl.BlockSpec((GB * rows, part), functools.partial(lambda f, i: (block_order(i, blocks, f), 0), flag))
        for flag in order_flags
    ]
    in_specs = [
        pl.BlockSpec((GB, 1, slots), lambda i: (shift + i, 0, 0)),
        pl.BlockSpec((experts, GB * cap, LANES), lambda i: (0, shift + i, 0)),
        pl.BlockSpec((experts, GB * cap, width), lambda i: (0, shift + i, 0)),
        pl.BlockSpec((GB * rows, units), lambda i: (shift + i, 0)),
        *token_specs,
        resident(gate_up.shape),
        resident(common_t.shape),
    ]
    operands = [slot_rows, slot_weights, dh, dhs, *streams, gate_up, common_t]
    aliases = {}
    if previous is not None:
        for at, value in enumerate(previous):
            aliases[len(operands)] = at
            in_specs.append(pl.BlockSpec(memory_space=pl.ANY))
            operands.append(value)
    return pl.pallas_call(
        body,
        grid=(blocks,),
        in_specs=in_specs,
        out_specs=[
            pl.BlockSpec((experts, GB * cap, D), lambda i: (0, shift + i, 0)),
            pl.BlockSpec((experts, GB * cap, width), lambda i: (0, shift + i, 0)),
            pl.BlockSpec((experts, GB * cap, double), lambda i: (0, shift + i, 0)),
            pl.BlockSpec((GB * rows, units), lambda i: (shift + i, 0)),
            pl.BlockSpec((GB * rows, 2 * units), lambda i: (shift + i, 0)),
        ],
        out_shape=[
            jax.ShapeDtypeStruct((experts, groups * cap, D), BF),
            jax.ShapeDtypeStruct((experts, groups * cap, width), BF),
            jax.ShapeDtypeStruct((experts, groups * cap, double), BF),
            jax.ShapeDtypeStruct((groups * rows, units), BF),
            jax.ShapeDtypeStruct((groups * rows, 2 * units), BF),
        ],
        input_output_aliases=aliases,
        compiler_params=pltpu.CompilerParams(vmem_limit_bytes=VMEM_CAP),
        name="expert_hidden",
    )(*operands)


def token_terms(half, order_flags, slot_rows, slot_values, weights, extra, extra_weights):
    groups, _, slots = slot_rows.shape
    experts, _, width = slot_values.shape
    cap = slots // experts
    rows = extra.shape[0] // groups
    units = extra.shape[1]
    blocks = groups // (2 * GB)
    shift = half * blocks
    count = len(order_flags)
    part = D // count

    def body(slot_ref, value_ref, weight_ref, extra_ref, extra_weight_ref, *out_refs):
        results = [dot(value_ref[j], weight_ref[j]).astype(BF) for j in range(experts)]
        for k in range(GB):
            stacked = jnp.concatenate([r[k * cap : (k + 1) * cap] for r in results], axis=0)
            total = dot(one_hot(slot_ref[k], rows), stacked) + dot(
                extra_ref[k * rows : (k + 1) * rows, :], extra_weight_ref[...]
            )
            for s in range(count):
                out_refs[s][k * rows : (k + 1) * rows, :] = total[
                    :, s * part : (s + 1) * part
                ].astype(BF)

    return pl.pallas_call(
        body,
        grid=(blocks,),
        in_specs=[
            pl.BlockSpec((GB, 1, slots), lambda i: (shift + i, 0, 0)),
            pl.BlockSpec((experts, GB * cap, width), lambda i: (0, shift + i, 0)),
            resident(weights.shape),
            pl.BlockSpec((GB * rows, units), lambda i: (shift + i, 0)),
            resident(extra_weights.shape),
        ],
        out_specs=[
            pl.BlockSpec(
                (GB * rows, part),
                functools.partial(lambda f, i: (block_order(i, blocks, f), 0), flag),
            )
            for flag in order_flags
        ],
        out_shape=[
            jax.ShapeDtypeStruct((groups // 2 * rows, part), BF) for _ in order_flags
        ],
        compiler_params=pltpu.CompilerParams(vmem_limit_bytes=VMEM_CAP),
        name="token_terms",
    )(slot_rows, slot_values, weights, extra, extra_weights)


def slot_tables(routes, route_weight, place_order, expert_total, capacity, padded):
    shard_rows = routes.shape[0]
    pair_count = shard_rows * TOPK
    expert_ids = routes.reshape(pair_count)
    ranks = place_order[0]
    earlier = (expert_ids[:, None] == expert_ids[None, :]) & (ranks[None, :] < ranks[:, None])
    places = jnp.sum(earlier.astype(jnp.int32), axis=1)
    slots = jnp.where(places < capacity, expert_ids * padded + places, -1)
    chosen = slots[:, None] == jnp.arange(expert_total * padded, dtype=jnp.int32)[None, :]
    pair_tokens = (jnp.arange(pair_count, dtype=jnp.int32) // TOPK).astype(F32)
    tokens = shard_rows + jnp.sum(
        jnp.where(chosen, pair_tokens[:, None] - shard_rows, 0.0), axis=0
    )
    weights = jnp.sum(jnp.where(chosen, route_weight.reshape(pair_count)[:, None], 0.0), axis=0)
    return jnp.stack([tokens, weights])


def norm_back(values, gain_row, grads):
    factor = lax.rsqrt(jnp.mean(values * values, axis=-1, keepdims=True) + NORM_EPS)
    scaled = gain_row * grads
    inner = jnp.mean(values * scaled, axis=-1, keepdims=True)
    grad_values = factor * scaled - values * (factor * factor * factor) * inner
    grad_gain = jnp.sum(grads * values * factor, axis=0)
    return grad_values, grad_gain


def local(
    layer_input,
    segment_ids,
    routes,
    route_weight,
    place_order,
    attention_gain,
    query_weight,
    latent_weight,
    latent_gain,
    latent_up,
    output_weight,
    experts_gain,
    expert_gate,
    expert_up,
    expert_down,
    shared_gate,
    shared_up,
    shared_down,
    out_cotangent,
):
    tensor_count = lax.axis_size("tensor")
    dp_count = lax.axis_size("dp")
    count = tensor_count * dp_count
    dp_at = lax.axis_index("dp")
    tensor_at = lax.axis_index("tensor")
    me = dp_at * tensor_count + tensor_at
    shard_rows = layer_input.shape[0]
    seq_len = segment_ids.shape[1]
    row_block = D // dp_count
    outer = [1 << b for b in range(count.bit_length() - 2, 0, -1)]
    order_a = tuple(outer)
    order_b = tuple(outer[:-2] + [outer[-1], outer[-2]])
    stream_orders = (order_a, order_b, order_a, order_b)
    order_flags = (False, True, False, True)
    part = D // len(stream_orders)
    tensor_masks = tuple(1 << b for b in range(tensor_count.bit_length() - 2, -1, -1))

    up_split = row_block // latent_up.shape[0]
    latent_pad = round_up(KV_RANK + QK_ROPE + 3, LANES)
    extras = jnp.concatenate(
        [
            latent_weight,
            attention_gain[:, None],
            experts_gain[:, None],
            jnp.broadcast_to(latent_gain[:, None], (latent_gain.shape[0], up_split)).reshape(-1, 1),
            jnp.zeros((row_block, latent_pad - KV_RANK - QK_ROPE - 3), BF),
        ],
        axis=1,
    )
    query_cols = query_weight.shape[1]
    out_cols = output_weight.shape[0]
    up_cols = latent_up.shape[1] // up_split
    packed = jnp.concatenate(
        [query_weight, output_weight.T, latent_up.reshape(row_block, up_cols), extras], axis=1
    )
    packed_full = lax.all_gather(packed, "dp", axis=0, tiled=True)
    hidden_total = shared_gate.shape[1]
    unit_block = hidden_total // tensor_count
    units = unit_block // dp_count
    unit_pad = round_up(units, LANES)
    column = tensor_at * unit_block
    common_send = jnp.stack(
        [
            lax.dynamic_slice_in_dim(shared_gate, column, unit_block, 1).T,
            lax.dynamic_slice_in_dim(shared_up, column, unit_block, 1).T,
            lax.dynamic_slice_in_dim(shared_down, column, unit_block, 0),
        ]
    ).reshape(3, dp_count, units, row_block)
    common_here = lax.all_to_all(
        jnp.transpose(common_send, (1, 0, 2, 3)), "dp", split_axis=0, concat_axis=0, tiled=True
    )
    common_here = jnp.transpose(common_here, (1, 2, 0, 3)).reshape(3, units, D)
    common_here = jnp.pad(common_here, ((0, 0), (0, unit_pad - units), (0, 0)))
    common_gu = common_here[:2].reshape(2 * unit_pad, D)
    common_down = common_here[2]
    common_gu_t = common_gu.T
    common_down_t = common_down.T

    expert_local = expert_gate.shape[0]
    expert_total = expert_local * dp_count
    capacity = max(2, 5 * shard_rows * TOPK // (4 * expert_total))
    padded = round_up(capacity, 16)
    slots = expert_local * padded
    tables = slot_tables(routes, route_weight, place_order, expert_total, capacity, padded)
    tables_all = cube_gather(tables[None], order_a + (CORE,), count)
    tables_mine = lax.dynamic_slice_in_dim(tables_all, dp_at * slots, slots, 2)
    relative = jnp.zeros((count,), jnp.int32)
    canon = jnp.arange(count, dtype=jnp.int32)
    for bit, mask in enumerate(order_a + (CORE,)):
        relative = relative + mask * ((canon >> bit) & 1)
    group_ids = me ^ relative
    slot_rows = tables_mine[:, :1, :].astype(jnp.int32)
    slot_weights = jnp.transpose(
        tables_mine[:, 1, :].reshape(count, expert_local, padded), (1, 0, 2)
    ).reshape(expert_local, count * padded, 1)
    slot_weights = jnp.broadcast_to(slot_weights, (expert_local, count * padded, LANES))

    width = expert_gate.shape[2]
    width_pad = round_up(width, LANES)
    pad_columns = ((0, 0), (0, 0), (0, width_pad - width))
    gate_up = jnp.concatenate(
        [jnp.pad(expert_gate, pad_columns), jnp.pad(expert_up, pad_columns)], axis=2
    )
    gate_up_t = jnp.transpose(gate_up, (0, 2, 1))
    down_pad = jnp.pad(expert_down, ((0, 0), (0, width_pad - width), (0, 0)))
    down_t = jnp.transpose(down_pad, (0, 2, 1))

    input_seq = cube_gather(layer_input, tensor_masks, count)
    ready = (gate_up, gate_up_t, down_pad, down_t, common_gu, common_gu_t, common_down, common_down_t)
    packed_full, (ready, slot_rows, slot_weights, input_seq) = tie(
        packed_full, (ready, slot_rows, slot_weights, input_seq)
    )
    gate_up, gate_up_t, down_pad, down_t, common_gu, common_gu_t, common_down, common_down_t = ready
    at = query_cols
    weight_query = packed_full[:, :at]
    weight_out_t = packed_full[:, at : at + out_cols]
    at += out_cols
    weight_up = packed_full[:, at : at + up_cols].reshape(KV_RANK, up_split * up_cols)
    at += up_cols
    weight_latent = packed_full[:, at : at + KV_RANK + QK_ROPE]
    at += KV_RANK + QK_ROPE
    mixer_scale = packed_full[:, at].astype(F32)
    experts_scale = packed_full[:, at + 1].astype(F32)
    latent_scale = packed_full[:, at + 2].reshape(KV_RANK, up_split)[:, 0].astype(F32)

    input_float = layer_input.astype(F32)
    hops = jnp.zeros((tensor_count,), jnp.int32)
    seq_blocks = jnp.arange(tensor_count, dtype=jnp.int32)
    for bit, mask in enumerate(tensor_masks):
        hops = hops + mask * ((seq_blocks >> bit) & 1)
    block_ids = tensor_at ^ hops
    positions = (
        block_ids[:, None] * shard_rows + jnp.arange(shard_rows, dtype=jnp.int32)[None, :]
    ).reshape(seq_len)
    doc_ids = jnp.take(segment_ids[0].reshape(tensor_count, shard_rows), block_ids, axis=0)
    doc_ids = doc_ids.reshape(seq_len)
    seq_cos, seq_sin = turn_tables(positions, QK_ROPE // 2)
    normed_full = root_norm(input_seq.astype(F32), mixer_scale).astype(BF)
    normed_first = normed_full[:shard_rows]
    latent_all = dot(normed_full, weight_latent)
    latent_full = root_norm(latent_all[:, :KV_RANK], latent_scale).astype(BF)
    rope_full = rotate(latent_all[:, KV_RANK:], seq_cos, seq_sin).astype(BF)
    latent_raw = latent_all[:shard_rows, :KV_RANK]
    head_dim = QK_NOPE + QK_ROPE
    local_heads = query_cols // head_dim
    query_raw = dot(normed_full, weight_query).reshape(seq_len, local_heads, head_dim)
    query_cat = jnp.concatenate(
        [
            query_raw[..., :QK_NOPE],
            rotate(query_raw[..., QK_NOPE:], seq_cos[:, None, :], seq_sin[:, None, :]),
        ],
        axis=-1,
    ).astype(BF)
    key_value = dot(latent_full, weight_up).astype(BF)
    key_value = key_value.reshape(seq_len, local_heads, QK_NOPE + V_DIM)
    key_rows = jnp.concatenate(
        [
            key_value[..., :QK_NOPE],
            jnp.broadcast_to(rope_full[:, None, :], (seq_len, local_heads, QK_ROPE)),
        ],
        axis=-1,
    )
    values = key_value[..., QK_NOPE:]
    scaling = head_dim ** (-0.5)
    raw_scores = jnp.einsum("qhd,khd->hqk", query_cat, key_rows, preferred_element_type=F32)
    raw_scores = raw_scores * scaling
    allowed = (doc_ids[:, None] == doc_ids[None, :]) & (positions[None, :] <= positions[:, None])
    masked = jnp.where(allowed[None], raw_scores, -1e30)
    row_max = jnp.max(masked, axis=-1, keepdims=True)
    exp_terms = jnp.exp(masked - row_max)
    row_total = jnp.sum(exp_terms, axis=-1, keepdims=True)
    prob_rows = exp_terms / row_total
    heads_out = jnp.einsum("hqk,khd->qhd", prob_rows.astype(BF), values, preferred_element_type=F32)
    heads_out = heads_out.astype(BF).reshape(seq_len, local_heads * V_DIM)
    mixer_terms = dot(heads_out, weight_out_t, ((1,), (1,)))
    mixer_out = scatter_rows(mixer_terms, tensor_masks[::-1], count)
    hidden_state = input_float + mixer_out
    normed_second = root_norm(hidden_state, experts_scale).astype(BF)

    cotangent_all = lax.all_gather(out_cotangent, BOTH, axis=0, tiled=True)
    grad_rows, grad_hidden, grad_hidden_common = cotangent_rows(
        group_ids, slot_rows, slot_weights, cotangent_all, down_t, common_down_t
    )

    near = [
        cube_gather(normed_second[:, s * part : (s + 1) * part], order[:-1], count)
        for s, order in enumerate(stream_orders)
    ]
    last = [swap_with(block, order[-1], count) for block, order in zip(near, stream_orders)]
    last, (grad_rows, grad_hidden, grad_hidden_common) = tie(
        last, (grad_rows, grad_hidden, grad_hidden_common)
    )
    near = [jnp.concatenate(pair, axis=0) for pair in zip(near, last)]
    far = [swap_with(block, CORE, count) for block in near]
    hidden_weights = (gate_up, common_gu_t)
    kept = None
    for half, streams in ((0, near), (1, far)):
        kept = expert_hidden(
            half, streams, order_flags, slot_rows, slot_weights, grad_hidden,
            grad_hidden_common, hidden_weights, kept,
        )
    rows_in, hidden_rows, grad_gu, hidden_common, grad_common = kept
    far_terms = token_terms(
        1, order_flags, slot_rows, grad_gu, gate_up_t, grad_common, common_gu
    )
    far_received = [swap_with(term, CORE, count) for term in far_terms]
    slot_rows_after, _ = tie(slot_rows, far_terms)
    near_terms = token_terms(
        0, order_flags, slot_rows_after, grad_gu, gate_up_t, grad_common, common_gu
    )

    def common_gradients(cotangents):
        half_rows = count // 2 * shard_rows
        parts = []
        for s, flag in enumerate(order_flags):
            total = 0.0
            for h, tokens in ((0, near[s]), (1, far[s])):
                grads = cotangents[h * half_rows : (h + 1) * half_rows]
                if flag:
                    shape = (2, 2, half_rows // 4, 2 * unit_pad)
                    grads = jnp.swapaxes(grads.reshape(shape), 0, 1).reshape(half_rows, 2 * unit_pad)
                total = total + dot(grads, tokens, ((0,), (0,)))
            parts.append(total)
        grad_common_gu = jnp.concatenate(parts, axis=1)
        return grad_common_gu

    if count > 32:
        grad_common_gu = common_gradients(grad_common)
        near_terms, grad_common_gu = tie(near_terms, grad_common_gu)
    turns = [order[::-1] for order in stream_orders]

    lower, sent, (slot_rows_late, rows_late, grad_gu_late, hidden_late) = halve_stage(
        near_terms, far_received, [turn[0] for turn in turns], count,
        (slot_rows, rows_in, grad_gu, hidden_rows),
    )

    def result_exchange(slot_rows_late):
        far_results = token_terms(
            1, order_flags, slot_rows_late, hidden_late, down_pad, hidden_common, common_down
        )
        far_results, slot_rows_late = tie(far_results, slot_rows_late)
        far_results_received = [swap_with(term, CORE, count) for term in far_results]
        near_results = token_terms(
            0, order_flags, slot_rows_late, hidden_late, down_pad, hidden_common, common_down
        )
        return near_results, far_results_received

    grad_expert_gate = jnp.stack(
        [dot(rows_late[j], grad_gu_late[j, :, :width], ((0,), (0,))) for j in range(expert_local)]
    )
    if count <= 32:
        near_results, far_results_received = result_exchange(slot_rows_late)
    lower, sent, (rows_late, grad_gu_late, hidden_late, grad_common_late) = halve_stage(
        lower, sent, [turn[1] for turn in turns], count,
        (rows_late, grad_gu_late, hidden_late, grad_common),
    )
    grad_expert_up = jnp.stack(
        [
            dot(rows_late[j], grad_gu_late[j, :, width_pad : width_pad + width], ((0,), (0,)))
            for j in range(expert_local)
        ]
    )
    if count <= 32:
        lower, sent, (near_results, hidden_late, grad_common_late) = halve_stage(
            lower, sent, [turn[2] for turn in turns], count,
            (near_results, hidden_late, grad_common_late),
        )
        grad_common_gu = common_gradients(grad_common_late)
        result_lower, result_sent, _ = halve_stage(
            near_results, far_results_received, [turn[0] for turn in turns], count
        )
    else:
        lower, sent, _ = halve_stage(lower, sent, [turn[2] for turn in turns], count)
    for k in range(3, len(order_a)):
        lower, sent, _ = halve_stage(lower, sent, [turn[k] for turn in turns], count)
    grad_normed_second = jnp.concatenate(
        [a + b.astype(F32) for a, b in zip(lower, sent)], axis=1
    )
    grad_expert_down = jnp.stack(
        [dot(hidden_late[j][:, :width], grad_rows[j], ((0,), (0,))) for j in range(expert_local)]
    )

    canon_ids = jnp.zeros((count,), jnp.int32)
    offset = me ^ canon
    for bit, mask in enumerate(order_a + (CORE,)):
        canon_ids = canon_ids + (1 << bit) * ((offset // mask) & 1)
    hidden_global = jnp.take(
        hidden_common.reshape(count, shard_rows, unit_pad), canon_ids, axis=0
    ).reshape(count * shard_rows, unit_pad)
    if count > 32:
        again, _ = tie(out_cotangent, grad_normed_second)
        cotangent_all = lax.all_gather(again, BOTH, axis=0, tiled=True)
    grad_common_down = dot(hidden_global, cotangent_all, ((0,), (0,)))
    common_grads = jnp.stack(
        [grad_common_gu[:units], grad_common_gu[unit_pad : unit_pad + units], grad_common_down[:units]]
    ).astype(BF)
    common_grads = jnp.transpose(
        common_grads.reshape(3, units, dp_count, row_block), (2, 0, 1, 3)
    )
    common_grads = lax.all_to_all(common_grads, "dp", split_axis=0, concat_axis=0, tiled=True)
    common_grads = jnp.transpose(common_grads, (1, 0, 2, 3)).reshape(3, unit_block, row_block)
    grad_shared_gate = common_grads[0].T.astype(F32)
    grad_shared_up = common_grads[1].T.astype(F32)
    grad_shared_down = common_grads[2].astype(F32)

    if count > 32:
        slot_rows_late, grad_normed_second = tie(slot_rows_late, grad_normed_second)
        near_results, far_results_received = result_exchange(slot_rows_late)
        result_lower, result_sent, _ = halve_stage(
            near_results, far_results_received, [turn[0] for turn in turns], count
        )
    cotangent = out_cotangent.astype(F32)
    grad_from_experts, grad_experts_part = norm_back(hidden_state, experts_scale, grad_normed_second)
    grad_hidden_state = cotangent + grad_from_experts
    grad_mixer_full = cube_gather(grad_hidden_state.astype(BF), tensor_masks, count)
    grad_output_t = dot(grad_mixer_full, heads_out, ((0,), (0,)))
    result_lower, result_sent, _ = halve_stage(
        result_lower, result_sent, [turn[1] for turn in turns], count
    )
    grad_output_t = lax.psum_scatter(
        grad_output_t.astype(BF), "dp", scatter_dimension=0, tiled=True
    )
    grad_heads = dot(grad_mixer_full, weight_out_t).astype(BF)
    grad_heads = grad_heads.reshape(seq_len, local_heads, V_DIM)
    grad_probs = jnp.einsum("qhd,khd->hqk", grad_heads, values, preferred_element_type=F32)
    row_dot = jnp.sum(prob_rows * grad_probs, axis=-1, keepdims=True)
    grad_scores = (prob_rows * (grad_probs - row_dot)).astype(BF)
    grad_query = scaling * jnp.einsum(
        "hqk,khd->qhd", grad_scores, key_rows, preferred_element_type=F32
    )
    grad_keys = scaling * jnp.einsum(
        "hqk,qhd->khd", grad_scores, query_cat, preferred_element_type=F32
    )
    grad_values = jnp.einsum(
        "hqk,qhd->khd", prob_rows.astype(BF), grad_heads, preferred_element_type=F32
    )
    grad_query_raw = (
        jnp.concatenate(
            [
                grad_query[..., :QK_NOPE],
                rotate(grad_query[..., QK_NOPE:], seq_cos[:, None, :], -seq_sin[:, None, :]),
            ],
            axis=-1,
        )
        .reshape(seq_len, local_heads * head_dim)
        .astype(BF)
    )
    grad_key_value = (
        jnp.concatenate([grad_keys[..., :QK_NOPE], grad_values], axis=-1)
        .reshape(seq_len, local_heads * (QK_NOPE + V_DIM))
        .astype(BF)
    )
    grad_terms = jnp.concatenate(
        [
            dot(grad_query_raw, weight_query, ((1,), (1,))).astype(BF),
            dot(grad_key_value, weight_up, ((1,), (1,))).astype(BF),
            jnp.sum(grad_keys[..., QK_NOPE:], axis=1).astype(BF),
            jnp.zeros((seq_len, QK_ROPE), BF),
        ],
        axis=1,
    )
    grad_shard = scatter_rows(grad_terms, tensor_masks[::-1], count)
    grad_shard, hidden_late = tie(grad_shard, hidden_state)
    result_lower, result_sent, _ = halve_stage(
        result_lower, result_sent, [turn[2] for turn in turns], count
    )
    grad_query_local = dot(normed_full, grad_query_raw, ((0,), (0,)))
    grad_up_local = dot(latent_full, grad_key_value, ((0,), (0,)))
    weight_terms = jnp.concatenate(
        [
            grad_query_local.astype(BF),
            grad_up_local.astype(BF).reshape(D, up_cols),
        ],
        axis=1,
    )
    weight_grads = lax.psum_scatter(weight_terms, "dp", scatter_dimension=0, tiled=True)
    weight_grads = weight_grads.astype(F32)
    grad_query_weight = weight_grads[:, :query_cols]
    grad_output_weight = grad_output_t.astype(F32).T
    grad_latent_up = weight_grads[:, query_cols:].reshape(latent_up.shape)

    grad_latent_raw, grad_latent_part = norm_back(
        latent_raw, latent_scale, grad_shard[:, D : D + KV_RANK]
    )
    grad_rope = rotate(
        grad_shard[:, D + KV_RANK : D + KV_RANK + QK_ROPE],
        seq_cos[:shard_rows],
        -seq_sin[:shard_rows],
    )
    grad_latent_all = jnp.concatenate([grad_latent_raw, grad_rope], axis=-1).astype(BF)
    grad_latent_local = dot(normed_first, grad_latent_all, ((0,), (0,)))
    grad_normed_first = grad_shard[:, :D] + dot(grad_latent_all, weight_latent, ((1,), (1,)))
    grad_from_mixer, grad_mixer_part = norm_back(input_float, mixer_scale, grad_normed_first)
    grad_input = grad_hidden_state + grad_from_mixer
    gain_rows = D // KV_RANK
    latent_part = jnp.pad(
        grad_latent_part.reshape(count, KV_RANK // count),
        ((0, 0), (0, (gain_rows - 1) * KV_RANK // count)),
    ).reshape(D, 1)
    small_terms = jnp.concatenate(
        [
            grad_latent_local,
            grad_mixer_part[:, None],
            grad_experts_part[:, None],
            latent_part,
            jnp.zeros((D, latent_pad - KV_RANK - QK_ROPE - 3), F32),
        ],
        axis=1,
    ).astype(BF)
    for k in range(3, len(order_a)):
        result_lower, result_sent, _ = halve_stage(
            result_lower, result_sent, [turn[k] for turn in turns], count
        )
    result = jnp.concatenate(
        [a + b.astype(F32) for a, b in zip(result_lower, result_sent)], axis=1
    )
    small_terms = jnp.take(small_terms.reshape(count, D // count, latent_pad), group_ids, axis=0)
    small_grads = scatter_rows(small_terms.reshape(D, latent_pad), (CORE,) + order_a[::-1], count)
    at = KV_RANK + QK_ROPE
    grad_latent_weight = small_grads[:, :at]
    grad_attention_gain = small_grads[:, at]
    grad_experts_gain = small_grads[:, at + 1]
    grad_latent_gain = small_grads[: KV_RANK // count, at + 2]
    layer_output = (hidden_late + result).astype(BF)
    return (
        layer_output,
        grad_input,
        grad_attention_gain,
        grad_query_weight,
        grad_latent_weight,
        grad_latent_gain,
        grad_latent_up,
        grad_output_weight,
        grad_experts_gain,
        grad_expert_gate,
        grad_expert_up,
        grad_expert_down,
        grad_shared_gate,
        grad_shared_up,
        grad_shared_down,
    )


def solution(mesh):
    return jax.shard_map(
        local,
        mesh=mesh,
        in_specs=(
            P(("dp", "tensor"), None),
            P("dp", None),
            P(("dp", "tensor"), None),
            P(("dp", "tensor"), None),
            P(("dp", "tensor"), None),
            P("dp"),
            P("dp", "tensor"),
            P("dp", None),
            P("dp"),
            P("dp", "tensor"),
            P("tensor", "dp"),
            P("dp"),
            P("dp", None, "tensor"),
            P("dp", None, "tensor"),
            P("dp", "tensor", None),
            P("dp", None),
            P("dp", None),
            P(None, "dp"),
            P(("dp", "tensor"), None),
        ),
        out_specs=(
            P(("dp", "tensor"), None),
            P(("dp", "tensor"), None),
            P(("dp", "tensor")),
            P("dp", "tensor"),
            P(("dp", "tensor"), None),
            P(("dp", "tensor")),
            P("dp", "tensor"),
            P("tensor", "dp"),
            P(("dp", "tensor")),
            P("dp", None, "tensor"),
            P("dp", None, "tensor"),
            P("dp", "tensor", None),
            P("dp", "tensor"),
            P("dp", "tensor"),
            P("tensor", "dp"),
        ),
        check_vma=False,
    )
```

```python
import functools

import jax
import jax.numpy as jnp
from jax import lax
from jax.experimental import pallas as pl
from jax.experimental.pallas import tpu as pltpu
from jax.sharding import PartitionSpec as P

D = 2048
QK_NOPE = 128
QK_ROPE = 64
V_DIM = 128
KV_RANK = 512
TOPK = 6
NORM_EPS = 1e-06

BF = jnp.bfloat16
F32 = jnp.float32
BOTH = ("dp", "tensor")
CORE = 1
GB = 4
LANES = 128
VMEM_CAP = 60 * 1024 * 1024


def round_up(value, step):
    return (value + step - 1) // step * step


def root_norm(values, gain_row):
    factor = lax.rsqrt(jnp.mean(values * values, axis=-1, keepdims=True) + NORM_EPS)
    return values * factor * gain_row


def turn_tables(positions, half_width):
    frequency = 10000.0 ** (-jnp.arange(half_width, dtype=F32) / half_width)
    angles = positions.astype(F32)[:, None] * frequency[None, :]
    return (jnp.cos(angles), jnp.sin(angles))


def rotate(values, cosine, sine_table):
    half_width = values.shape[-1] // 2
    first_half = values[..., :half_width]
    second_half = values[..., half_width:]
    return jnp.concatenate(
        [
            first_half * cosine - second_half * sine_table,
            first_half * sine_table + second_half * cosine,
        ],
        axis=-1,
    )


def dot(left, right, dims=((1,), (0,))):
    return lax.dot_general(left, right, (dims, ((), ())), preferred_element_type=F32)


def swap_with(values, mask, count):
    return lax.ppermute(values, BOTH, [(i, i ^ mask) for i in range(count)])


def cube_gather(block, masks, count):
    for mask in masks:
        block = jnp.concatenate([block, swap_with(block, mask, count)], axis=0)
    return block


def tie(first, second):
    return lax.optimization_barrier((first, second))


def halve_stage(keeps, receiveds, masks, count, follow=()):
    half = keeps[0].shape[0] // 2
    upper = [
        (k[half:].astype(F32) + r[half:].astype(F32)).astype(BF)
        for k, r in zip(keeps, receiveds)
    ]
    first, follow = tie(upper[:2], follow)
    upper = [*first, *upper[2:]]
    sent = [swap_with(value, mask, count) for value, mask in zip(upper, masks)]
    lower = [
        (k[:half].astype(F32) + r[:half].astype(F32)).astype(BF)
        for k, r in zip(keeps, receiveds)
    ]
    return lower, sent, follow


def scatter_rows(partial, masks, count):
    for mask in masks:
        half = partial.shape[0] // 2
        received = swap_with(partial[half:].astype(BF), mask, count)
        partial = partial[:half].astype(F32) + received.astype(F32)
    return partial


def block_order(block, blocks, swapped):
    if not swapped:
        return block
    top, low = block // (blocks // 2), (block // (blocks // 4)) % 2
    return low * (blocks // 2) + top * (blocks // 4) + block % (blocks // 4)


def one_hot(slot_row, rows):
    tokens = lax.broadcasted_iota(jnp.int32, (rows, slot_row.shape[1]), 0)
    return jnp.where(tokens == slot_row, 1.0, 0.0).astype(BF)


def resident(shape):
    return pl.BlockSpec(shape, lambda *_: (0,) * len(shape), pipeline_mode=pl.Buffered(1))


def cotangent_rows(half, streams, slot_rows, slot_weights, down_t, common_down_t, previous):
    groups, _, slots = slot_rows.shape
    experts, _, width = down_t.shape
    cap = slots // experts
    blocks = groups // (2 * GB)
    rows = streams[0].shape[0] // (groups // 2)
    part = streams[0].shape[1]
    units = common_down_t.shape[1]
    count = len(streams)

    def body(*refs):
        slot_ref, weight_ref = refs[:2]
        token_refs = refs[2 : 2 + count]
        down_ref, common_ref = refs[2 + count : 4 + count]
        rows_ref, dh_ref, dhs_ref = refs[-3:]
        for k in range(GB):
            picks = one_hot(slot_ref[k], rows)
            for s in range(count):
                picked = dot(
                    picks, token_refs[s][k * rows : (k + 1) * rows, :], ((0,), (0,))
                ).astype(BF)
                for j in range(experts):
                    rows_ref[j, k * cap : (k + 1) * cap, s * part : (s + 1) * part] = picked[
                        j * cap : (j + 1) * cap
                    ]
        total = dot(token_refs[0][...], common_ref[:part, :])
        for s in range(1, count):
            total += dot(token_refs[s][...], common_ref[s * part : (s + 1) * part, :])
        dhs_ref[...] = total
        for j in range(experts):
            dh_ref[j] = dot(rows_ref[j], down_ref[j]) * weight_ref[j][:, :1]

    shift = half * blocks
    in_specs = [
        pl.BlockSpec((GB, 1, slots), lambda i: (shift + i, 0, 0)),
        pl.BlockSpec((experts, GB * cap, LANES), lambda i: (0, shift + i, 0)),
        *[pl.BlockSpec((GB * rows, part), lambda i: (i, 0)) for _ in streams],
        resident(down_t.shape),
        resident(common_down_t.shape),
    ]
    operands = [slot_rows, slot_weights, *streams, down_t, common_down_t]
    aliases = {}
    if previous is not None:
        for at, value in enumerate(previous):
            aliases[len(operands)] = at
            in_specs.append(pl.BlockSpec(memory_space=pl.ANY))
            operands.append(value)
    return pl.pallas_call(
        body,
        grid=(blocks,),
        in_specs=in_specs,
        out_specs=[
            pl.BlockSpec((experts, GB * cap, D), lambda i: (0, shift + i, 0)),
            pl.BlockSpec((experts, GB * cap, width), lambda i: (0, shift + i, 0)),
            pl.BlockSpec((GB * rows, units), lambda i: (shift + i, 0)),
        ],
        out_shape=[
            jax.ShapeDtypeStruct((experts, groups * cap, D), BF),
            jax.ShapeDtypeStruct((experts, groups * cap, width), F32),
            jax.ShapeDtypeStruct((groups * rows, units), F32),
        ],
        input_output_aliases=aliases,
        compiler_params=pltpu.CompilerParams(vmem_limit_bytes=VMEM_CAP),
        name="cotangent_rows",
    )(*operands)


def expert_hidden(half, streams, order_flags, slot_rows, slot_weights, dh, dhs, weights, previous):
    gate_up, common_t = weights
    groups, _, slots = slot_rows.shape
    experts, _, double = gate_up.shape
    width = double // 2
    cap = slots // experts
    blocks = groups // (2 * GB)
    rows = streams[0].shape[0] // (groups // 2)
    part = streams[0].shape[1]
    units = dhs.shape[1]
    count = len(streams)

    def body(*refs):
        slot_ref, weight_ref, dh_ref, dhs_ref = refs[:4]
        token_refs = refs[4 : 4 + count]
        gu_ref, common_t_ref = refs[4 + count : 6 + count]
        x_ref, hidden_ref, dgu_ref, hs_ref, dgs_ref = refs[-5:]
        for k in range(GB):
            picks = one_hot(slot_ref[k], rows)
            for s in range(count):
                picked = dot(
                    picks, token_refs[s][k * rows : (k + 1) * rows, :], ((0,), (0,))
                ).astype(BF)
                for j in range(experts):
                    x_ref[j, k * cap : (k + 1) * cap, s * part : (s + 1) * part] = picked[
                        j * cap : (j + 1) * cap
                    ]
        common_gu = dot(token_refs[0][...], common_t_ref[:part, :])
        for s in range(1, count):
            common_gu += dot(token_refs[s][...], common_t_ref[s * part : (s + 1) * part, :])
        gate, up = common_gu[:, :units], common_gu[:, units:]
        logistic = jax.nn.sigmoid(gate)
        silu = gate * logistic
        hs_ref[...] = (silu * up).astype(BF)
        grad_hidden = dhs_ref[...]
        slope = logistic * (1.0 + gate * (1.0 - logistic))
        dgs_ref[:, :units] = (grad_hidden * up * slope).astype(BF)
        dgs_ref[:, units:] = (grad_hidden * silu).astype(BF)
        for j in range(experts):
            both = dot(x_ref[j], gu_ref[j])
            gate, up = both[:, :width], both[:, width:]
            logistic = jax.nn.sigmoid(gate)
            silu = gate * logistic
            hidden_ref[j] = (silu * up * weight_ref[j][:, :1]).astype(BF)
            grad_hidden = dh_ref[j]
            slope = logistic * (1.0 + gate * (1.0 - logistic))
            dgu_ref[j, :, :width] = (grad_hidden * up * slope).astype(BF)
            dgu_ref[j, :, width:] = (grad_hidden * silu).astype(BF)

    shift = half * blocks
    token_specs = [
        pl.BlockSpec((GB * rows, part), functools.partial(lambda f, i: (block_order(i, blocks, f), 0), flag))
        for flag in order_flags
    ]
    in_specs = [
        pl.BlockSpec((GB, 1, slots), lambda i: (shift + i, 0, 0)),
        pl.BlockSpec((experts, GB * cap, LANES), lambda i: (0, shift + i, 0)),
        pl.BlockSpec((experts, GB * cap, width), lambda i: (0, shift + i, 0)),
        pl.BlockSpec((GB * rows, units), lambda i: (shift + i, 0)),
        *token_specs,
        resident(gate_up.shape),
        resident(common_t.shape),
    ]
    operands = [slot_rows, slot_weights, dh, dhs, *streams, gate_up, common_t]
    aliases = {}
    if previous is not None:
        for at, value in enumerate(previous):
            aliases[len(operands)] = at
            in_specs.append(pl.BlockSpec(memory_space=pl.ANY))
            operands.append(value)
    return pl.pallas_call(
        body,
        grid=(blocks,),
        in_specs=in_specs,
        out_specs=[
            pl.BlockSpec((experts, GB * cap, D), lambda i: (0, shift + i, 0)),
            pl.BlockSpec((experts, GB * cap, width), lambda i: (0, shift + i, 0)),
            pl.BlockSpec((experts, GB * cap, double), lambda i: (0, shift + i, 0)),
            pl.BlockSpec((GB * rows, units), lambda i: (shift + i, 0)),
            pl.BlockSpec((GB * rows, 2 * units), lambda i: (shift + i, 0)),
        ],
        out_shape=[
            jax.ShapeDtypeStruct((experts, groups * cap, D), BF),
            jax.ShapeDtypeStruct((experts, groups * cap, width), BF),
            jax.ShapeDtypeStruct((experts, groups * cap, double), BF),
            jax.ShapeDtypeStruct((groups * rows, units), BF),
            jax.ShapeDtypeStruct((groups * rows, 2 * units), BF),
        ],
        input_output_aliases=aliases,
        compiler_params=pltpu.CompilerParams(vmem_limit_bytes=VMEM_CAP),
        name="expert_hidden",
    )(*operands)


def token_terms(half, order_flags, slot_rows, slot_values, weights, extra, extra_weights):
    groups, _, slots = slot_rows.shape
    experts, _, width = slot_values.shape
    cap = slots // experts
    rows = extra.shape[0] // groups
    units = extra.shape[1]
    blocks = groups // (2 * GB)
    shift = half * blocks
    count = len(order_flags)
    part = D // count

    def body(slot_ref, value_ref, weight_ref, extra_ref, extra_weight_ref, *out_refs):
        results = [dot(value_ref[j], weight_ref[j]).astype(BF) for j in range(experts)]
        for k in range(GB):
            stacked = jnp.concatenate([r[k * cap : (k + 1) * cap] for r in results], axis=0)
            total = dot(one_hot(slot_ref[k], rows), stacked) + dot(
                extra_ref[k * rows : (k + 1) * rows, :], extra_weight_ref[...]
            )
            for s in range(count):
                out_refs[s][k * rows : (k + 1) * rows, :] = total[
                    :, s * part : (s + 1) * part
                ].astype(BF)

    return pl.pallas_call(
        body,
        grid=(blocks,),
        in_specs=[
            pl.BlockSpec((GB, 1, slots), lambda i: (shift + i, 0, 0)),
            pl.BlockSpec((experts, GB * cap, width), lambda i: (0, shift + i, 0)),
            resident(weights.shape),
            pl.BlockSpec((GB * rows, units), lambda i: (shift + i, 0)),
            resident(extra_weights.shape),
        ],
        out_specs=[
            pl.BlockSpec(
                (GB * rows, part),
                functools.partial(lambda f, i: (block_order(i, blocks, f), 0), flag),
            )
            for flag in order_flags
        ],
        out_shape=[
            jax.ShapeDtypeStruct((groups // 2 * rows, part), BF) for _ in order_flags
        ],
        compiler_params=pltpu.CompilerParams(vmem_limit_bytes=VMEM_CAP),
        name="token_terms",
    )(slot_rows, slot_values, weights, extra, extra_weights)


def slot_tables(routes, route_weight, place_order, expert_total, capacity, padded):
    shard_rows = routes.shape[0]
    pair_count = shard_rows * TOPK
    expert_ids = routes.reshape(pair_count)
    ranks = place_order[0]
    earlier = (expert_ids[:, None] == expert_ids[None, :]) & (ranks[None, :] < ranks[:, None])
    places = jnp.sum(earlier.astype(jnp.int32), axis=1)
    slots = jnp.where(places < capacity, expert_ids * padded + places, -1)
    chosen = slots[:, None] == jnp.arange(expert_total * padded, dtype=jnp.int32)[None, :]
    pair_tokens = (jnp.arange(pair_count, dtype=jnp.int32) // TOPK).astype(F32)
    tokens = shard_rows + jnp.sum(
        jnp.where(chosen, pair_tokens[:, None] - shard_rows, 0.0), axis=0
    )
    weights = jnp.sum(jnp.where(chosen, route_weight.reshape(pair_count)[:, None], 0.0), axis=0)
    return jnp.stack([tokens, weights])


def norm_back(values, gain_row, grads):
    factor = lax.rsqrt(jnp.mean(values * values, axis=-1, keepdims=True) + NORM_EPS)
    scaled = gain_row * grads
    inner = jnp.mean(values * scaled, axis=-1, keepdims=True)
    grad_values = factor * scaled - values * (factor * factor * factor) * inner
    grad_gain = jnp.sum(grads * values * factor, axis=0)
    return grad_values, grad_gain


def local(
    layer_input,
    segment_ids,
    routes,
    route_weight,
    place_order,
    attention_gain,
    query_weight,
    latent_weight,
    latent_gain,
    latent_up,
    output_weight,
    experts_gain,
    expert_gate,
    expert_up,
    expert_down,
    shared_gate,
    shared_up,
    shared_down,
    out_cotangent,
):
    tensor_count = lax.axis_size("tensor")
    dp_count = lax.axis_size("dp")
    count = tensor_count * dp_count
    dp_at = lax.axis_index("dp")
    tensor_at = lax.axis_index("tensor")
    me = dp_at * tensor_count + tensor_at
    shard_rows = layer_input.shape[0]
    seq_len = segment_ids.shape[1]
    row_block = D // dp_count
    outer = [1 << b for b in range(count.bit_length() - 2, 0, -1)]
    order_a = tuple(outer)
    order_b = tuple(outer[:-2] + [outer[-1], outer[-2]])
    stream_orders = (order_a, order_b, order_a, order_b)
    order_flags = (False, True, False, True)
    part = D // len(stream_orders)
    tensor_masks = tuple(1 << b for b in range(tensor_count.bit_length() - 2, -1, -1))

    up_split = row_block // latent_up.shape[0]
    latent_pad = round_up(KV_RANK + QK_ROPE + 3, LANES)
    extras = jnp.concatenate(
        [
            latent_weight,
            attention_gain[:, None],
            experts_gain[:, None],
            jnp.broadcast_to(latent_gain[:, None], (latent_gain.shape[0], up_split)).reshape(-1, 1),
            jnp.zeros((row_block, latent_pad - KV_RANK - QK_ROPE - 3), BF),
        ],
        axis=1,
    )
    query_cols = query_weight.shape[1]
    out_cols = output_weight.shape[0]
    up_cols = latent_up.shape[1] // up_split
    packed = jnp.concatenate(
        [query_weight, output_weight.T, latent_up.reshape(row_block, up_cols), extras], axis=1
    )
    packed_full = lax.all_gather(packed, "dp", axis=0, tiled=True)
    hidden_total = shared_gate.shape[1]
    unit_block = hidden_total // tensor_count
    units = unit_block // dp_count
    unit_pad = round_up(units, LANES)
    column = tensor_at * unit_block
    common_send = jnp.stack(
        [
            lax.dynamic_slice_in_dim(shared_gate, column, unit_block, 1).T,
            lax.dynamic_slice_in_dim(shared_up, column, unit_block, 1).T,
            lax.dynamic_slice_in_dim(shared_down, column, unit_block, 0),
        ]
    ).reshape(3, dp_count, units, row_block)
    common_here = lax.all_to_all(
        jnp.transpose(common_send, (1, 0, 2, 3)), "dp", split_axis=0, concat_axis=0, tiled=True
    )
    common_here = jnp.transpose(common_here, (1, 2, 0, 3)).reshape(3, units, D)
    common_here = jnp.pad(common_here, ((0, 0), (0, unit_pad - units), (0, 0)))
    common_gu = common_here[:2].reshape(2 * unit_pad, D)
    common_down = common_here[2]
    common_gu_t = common_gu.T
    common_down_t = common_down.T

    cotangent_part = D // 2

    def first_cotangents(source):
        return [
            cube_gather(
                source[:, s * cotangent_part : (s + 1) * cotangent_part], order_a[:-1], count
            )
            for s in range(2)
        ]

    def last_cotangents(blocks):
        near = [cube_gather(block, order_a[-1:], count) for block in blocks]
        return near, [swap_with(block, CORE, count) for block in near]

    cotangent_blocks = first_cotangents(out_cotangent)

    expert_local = expert_gate.shape[0]
    expert_total = expert_local * dp_count
    capacity = max(2, 5 * shard_rows * TOPK // (4 * expert_total))
    padded = round_up(capacity, 16)
    slots = expert_local * padded
    tables = slot_tables(routes, route_weight, place_order, expert_total, capacity, padded)
    tables_all = cube_gather(tables[None], order_a + (CORE,), count)
    tables_mine = lax.dynamic_slice_in_dim(tables_all, dp_at * slots, slots, 2)
    relative = jnp.zeros((count,), jnp.int32)
    canon = jnp.arange(count, dtype=jnp.int32)
    for bit, mask in enumerate(order_a + (CORE,)):
        relative = relative + mask * ((canon >> bit) & 1)
    group_ids = me ^ relative
    slot_rows = tables_mine[:, :1, :].astype(jnp.int32)
    slot_weights = jnp.transpose(
        tables_mine[:, 1, :].reshape(count, expert_local, padded), (1, 0, 2)
    ).reshape(expert_local, count * padded, 1)
    slot_weights = jnp.broadcast_to(slot_weights, (expert_local, count * padded, LANES))

    width = expert_gate.shape[2]
    width_pad = round_up(width, LANES)
    pad_columns = ((0, 0), (0, 0), (0, width_pad - width))
    gate_up = jnp.concatenate(
        [jnp.pad(expert_gate, pad_columns), jnp.pad(expert_up, pad_columns)], axis=2
    )
    gate_up_t = jnp.transpose(gate_up, (0, 2, 1))
    down_pad = jnp.pad(expert_down, ((0, 0), (0, width_pad - width), (0, 0)))
    down_t = jnp.transpose(down_pad, (0, 2, 1))

    input_seq = cube_gather(layer_input, tensor_masks, count)
    ready = (gate_up, gate_up_t, down_pad, down_t, common_gu, common_gu_t, common_down, common_down_t)
    packed_full, (ready, slot_rows, slot_weights, input_seq) = tie(
        packed_full, (ready, slot_rows, slot_weights, input_seq)
    )
    if count <= 32:
        packed_full, cotangent_blocks[1] = tie(packed_full, cotangent_blocks[1])
    cotangents_near, cotangents_far = last_cotangents(cotangent_blocks)
    gate_up, gate_up_t, down_pad, down_t, common_gu, common_gu_t, common_down, common_down_t = ready
    at = query_cols
    weight_query = packed_full[:, :at]
    weight_out_t = packed_full[:, at : at + out_cols]
    at += out_cols
    weight_up = packed_full[:, at : at + up_cols].reshape(KV_RANK, up_split * up_cols)
    at += up_cols
    weight_latent = packed_full[:, at : at + KV_RANK + QK_ROPE]
    at += KV_RANK + QK_ROPE
    mixer_scale = packed_full[:, at].astype(F32)
    experts_scale = packed_full[:, at + 1].astype(F32)
    latent_scale = packed_full[:, at + 2].reshape(KV_RANK, up_split)[:, 0].astype(F32)

    input_float = layer_input.astype(F32)
    hops = jnp.zeros((tensor_count,), jnp.int32)
    seq_blocks = jnp.arange(tensor_count, dtype=jnp.int32)
    for bit, mask in enumerate(tensor_masks):
        hops = hops + mask * ((seq_blocks >> bit) & 1)
    block_ids = tensor_at ^ hops
    positions = (
        block_ids[:, None] * shard_rows + jnp.arange(shard_rows, dtype=jnp.int32)[None, :]
    ).reshape(seq_len)
    doc_ids = jnp.take(segment_ids[0].reshape(tensor_count, shard_rows), block_ids, axis=0)
    doc_ids = doc_ids.reshape(seq_len)
    seq_cos, seq_sin = turn_tables(positions, QK_ROPE // 2)
    normed_full = root_norm(input_seq.astype(F32), mixer_scale).astype(BF)
    normed_first = normed_full[:shard_rows]
    latent_all = dot(normed_full, weight_latent)
    latent_full = root_norm(latent_all[:, :KV_RANK], latent_scale).astype(BF)
    rope_full = rotate(latent_all[:, KV_RANK:], seq_cos, seq_sin).astype(BF)
    latent_raw = latent_all[:shard_rows, :KV_RANK]
    head_dim = QK_NOPE + QK_ROPE
    local_heads = query_cols // head_dim
    query_raw = dot(normed_full, weight_query).reshape(seq_len, local_heads, head_dim)
    query_cat = jnp.concatenate(
        [
            query_raw[..., :QK_NOPE],
            rotate(query_raw[..., QK_NOPE:], seq_cos[:, None, :], seq_sin[:, None, :]),
        ],
        axis=-1,
    ).astype(BF)
    key_value = dot(latent_full, weight_up).astype(BF)
    key_value = key_value.reshape(seq_len, local_heads, QK_NOPE + V_DIM)
    key_rows = jnp.concatenate(
        [
            key_value[..., :QK_NOPE],
            jnp.broadcast_to(rope_full[:, None, :], (seq_len, local_heads, QK_ROPE)),
        ],
        axis=-1,
    )
    values = key_value[..., QK_NOPE:]
    scaling = head_dim ** (-0.5)
    raw_scores = jnp.einsum("qhd,khd->hqk", query_cat, key_rows, preferred_element_type=F32)
    raw_scores = raw_scores * scaling
    allowed = (doc_ids[:, None] == doc_ids[None, :]) & (positions[None, :] <= positions[:, None])
    masked = jnp.where(allowed[None], raw_scores, -1e30)
    row_max = jnp.max(masked, axis=-1, keepdims=True)
    exp_terms = jnp.exp(masked - row_max)
    row_total = jnp.sum(exp_terms, axis=-1, keepdims=True)
    prob_rows = exp_terms / row_total
    heads_out = jnp.einsum("hqk,khd->qhd", prob_rows.astype(BF), values, preferred_element_type=F32)
    heads_out = heads_out.astype(BF).reshape(seq_len, local_heads * V_DIM)
    mixer_terms = dot(heads_out, weight_out_t, ((1,), (1,)))
    mixer_out = scatter_rows(mixer_terms, tensor_masks[::-1], count)
    hidden_state = input_float + mixer_out
    normed_second = root_norm(hidden_state, experts_scale).astype(BF)

    cotangent_kept = None
    for half, streams in ((0, cotangents_near), (1, cotangents_far)):
        cotangent_kept = cotangent_rows(
            half, streams, slot_rows, slot_weights, down_t, common_down_t, cotangent_kept
        )
    grad_rows, grad_hidden, grad_hidden_common = cotangent_kept

    near = [
        cube_gather(normed_second[:, s * part : (s + 1) * part], order, count)
        for s, order in enumerate(stream_orders)
    ]
    far = [swap_with(block, CORE, count) for block in near]
    hidden_weights = (gate_up, common_gu_t)
    kept = None
    for half, streams in ((0, near), (1, far)):
        kept = expert_hidden(
            half, streams, order_flags, slot_rows, slot_weights, grad_hidden,
            grad_hidden_common, hidden_weights, kept,
        )
    rows_in, hidden_rows, grad_gu, hidden_common, grad_common = kept
    far_terms = token_terms(
        1, order_flags, slot_rows, grad_gu, gate_up_t, grad_common, common_gu
    )
    far_received = [swap_with(term, CORE, count) for term in far_terms]
    slot_rows_after, _ = tie(slot_rows, far_terms)
    near_terms = token_terms(
        0, order_flags, slot_rows_after, grad_gu, gate_up_t, grad_common, common_gu
    )

    def common_gradients(cotangents):
        half_rows = count // 2 * shard_rows
        parts = []
        for s, flag in enumerate(order_flags):
            total = 0.0
            for h, tokens in ((0, near[s]), (1, far[s])):
                grads = cotangents[h * half_rows : (h + 1) * half_rows]
                if flag:
                    shape = (2, 2, half_rows // 4, 2 * unit_pad)
                    grads = jnp.swapaxes(grads.reshape(shape), 0, 1).reshape(half_rows, 2 * unit_pad)
                total = total + dot(grads, tokens, ((0,), (0,)))
            parts.append(total)
        return jnp.concatenate(parts, axis=1)

    def common_down_gradient(hidden):
        half_rows = count // 2 * shard_rows
        return jnp.concatenate(
            [
                dot(hidden[:half_rows], cotangents_near[s], ((0,), (0,)))
                + dot(hidden[half_rows:], cotangents_far[s], ((0,), (0,)))
                for s in range(2)
            ],
            axis=1,
        )

    if count > 32:
        grad_common_gu = common_gradients(grad_common)
        near_terms, grad_common_gu = tie(near_terms, grad_common_gu)
    turns = [order[::-1] for order in stream_orders]

    lower, sent, (slot_rows_late, rows_late, grad_gu_late, hidden_late) = halve_stage(
        near_terms, far_received, [turn[0] for turn in turns], count,
        (slot_rows, rows_in, grad_gu, hidden_rows),
    )

    def result_exchange(slot_rows_late):
        far_results = token_terms(
            1, order_flags, slot_rows_late, hidden_late, down_pad, hidden_common, common_down
        )
        far_results, slot_rows_late = tie(far_results, slot_rows_late)
        far_results_received = [swap_with(term, CORE, count) for term in far_results]
        near_results = token_terms(
            0, order_flags, slot_rows_late, hidden_late, down_pad, hidden_common, common_down
        )
        return near_results, far_results_received

    grad_expert_gate = jnp.stack(
        [dot(rows_late[j], grad_gu_late[j, :, :width], ((0,), (0,))) for j in range(expert_local)]
    )
    if count <= 32:
        near_results, far_results_received = result_exchange(slot_rows_late)
    lower, sent, (rows_late, grad_gu_late, hidden_late, grad_common_late) = halve_stage(
        lower, sent, [turn[1] for turn in turns], count,
        (rows_late, grad_gu_late, hidden_late, grad_common),
    )
    grad_expert_up = jnp.stack(
        [
            dot(rows_late[j], grad_gu_late[j, :, width_pad : width_pad + width], ((0,), (0,)))
            for j in range(expert_local)
        ]
    )
    if count <= 32:
        lower, sent, (near_results, hidden_late, grad_common_late) = halve_stage(
            lower, sent, [turn[2] for turn in turns], count,
            (near_results, hidden_late, grad_common_late),
        )
        grad_common_gu = common_gradients(grad_common_late)
        grad_common_down = common_down_gradient(hidden_common)
        result_lower, result_sent, _ = halve_stage(
            near_results, far_results_received, [turn[0] for turn in turns], count
        )
    else:
        lower, sent, _ = halve_stage(lower, sent, [turn[2] for turn in turns], count)
    for k in range(3, len(order_a)):
        lower, sent, _ = halve_stage(lower, sent, [turn[k] for turn in turns], count)
    grad_normed_second = jnp.concatenate(
        [a.astype(F32) + b.astype(F32) for a, b in zip(lower, sent)], axis=1
    )
    grad_expert_down = jnp.stack(
        [dot(hidden_late[j][:, :width], grad_rows[j], ((0,), (0,))) for j in range(expert_local)]
    )

    if count > 32:
        again, grad_normed_second = tie(out_cotangent, grad_normed_second)
        cotangents_near, cotangents_far = last_cotangents(first_cotangents(again))
        grad_common_down = common_down_gradient(hidden_common)
    common_grads = jnp.stack(
        [grad_common_gu[:units], grad_common_gu[unit_pad : unit_pad + units], grad_common_down[:units]]
    ).astype(BF)
    common_grads = jnp.transpose(
        common_grads.reshape(3, units, dp_count, row_block), (2, 0, 1, 3)
    )
    common_grads = lax.all_to_all(common_grads, "dp", split_axis=0, concat_axis=0, tiled=True)
    common_grads = jnp.transpose(common_grads, (1, 0, 2, 3)).reshape(3, unit_block, row_block)
    grad_shared_gate = common_grads[0].T.astype(F32)
    grad_shared_up = common_grads[1].T.astype(F32)
    grad_shared_down = common_grads[2].astype(F32)

    if count > 32:
        slot_rows_late, grad_normed_second = tie(slot_rows_late, grad_normed_second)
        near_results, far_results_received = result_exchange(slot_rows_late)
        result_lower, result_sent, _ = halve_stage(
            near_results, far_results_received, [turn[0] for turn in turns], count
        )
    cotangent = out_cotangent.astype(F32)
    grad_from_experts, grad_experts_part = norm_back(hidden_state, experts_scale, grad_normed_second)
    grad_hidden_state = cotangent + grad_from_experts
    grad_mixer_full = cube_gather(grad_hidden_state.astype(BF), tensor_masks, count)
    grad_output_t = dot(grad_mixer_full, heads_out, ((0,), (0,)))
    result_lower, result_sent, _ = halve_stage(
        result_lower, result_sent, [turn[1] for turn in turns], count
    )
    grad_output_t = lax.psum_scatter(
        grad_output_t.astype(BF), "dp", scatter_dimension=0, tiled=True
    )
    grad_heads = dot(grad_mixer_full, weight_out_t).astype(BF)
    grad_heads = grad_heads.reshape(seq_len, local_heads, V_DIM)
    grad_probs = jnp.einsum("qhd,khd->hqk", grad_heads, values, preferred_element_type=F32)
    row_dot = jnp.sum(prob_rows * grad_probs, axis=-1, keepdims=True)
    grad_scores = (prob_rows * (grad_probs - row_dot)).astype(BF)
    grad_query = scaling * jnp.einsum(
        "hqk,khd->qhd", grad_scores, key_rows, preferred_element_type=F32
    )
    grad_keys = scaling * jnp.einsum(
        "hqk,qhd->khd", grad_scores, query_cat, preferred_element_type=F32
    )
    grad_values = jnp.einsum(
        "hqk,qhd->khd", prob_rows.astype(BF), grad_heads, preferred_element_type=F32
    )
    grad_query_raw = (
        jnp.concatenate(
            [
                grad_query[..., :QK_NOPE],
                rotate(grad_query[..., QK_NOPE:], seq_cos[:, None, :], -seq_sin[:, None, :]),
            ],
            axis=-1,
        )
        .reshape(seq_len, local_heads * head_dim)
        .astype(BF)
    )
    grad_key_value = (
        jnp.concatenate([grad_keys[..., :QK_NOPE], grad_values], axis=-1)
        .reshape(seq_len, local_heads * (QK_NOPE + V_DIM))
        .astype(BF)
    )
    grad_terms = jnp.concatenate(
        [
            dot(grad_query_raw, weight_query, ((1,), (1,))).astype(BF),
            dot(grad_key_value, weight_up, ((1,), (1,))).astype(BF),
            jnp.sum(grad_keys[..., QK_NOPE:], axis=1).astype(BF),
            jnp.zeros((seq_len, QK_ROPE), BF),
        ],
        axis=1,
    )
    grad_shard = scatter_rows(grad_terms, tensor_masks[::-1], count)
    grad_shard, hidden_late = tie(grad_shard, hidden_state)
    result_lower, result_sent, _ = halve_stage(
        result_lower, result_sent, [turn[2] for turn in turns], count
    )
    grad_query_local = dot(normed_full, grad_query_raw, ((0,), (0,)))
    grad_up_local = dot(latent_full, grad_key_value, ((0,), (0,)))
    weight_terms = jnp.concatenate(
        [
            grad_query_local.astype(BF),
            grad_up_local.astype(BF).reshape(D, up_cols),
        ],
        axis=1,
    )
    weight_grads = lax.psum_scatter(weight_terms, "dp", scatter_dimension=0, tiled=True)
    weight_grads = weight_grads.astype(F32)
    grad_query_weight = weight_grads[:, :query_cols]
    grad_output_weight = grad_output_t.astype(F32).T
    grad_latent_up = weight_grads[:, query_cols:].reshape(latent_up.shape)

    grad_latent_raw, grad_latent_part = norm_back(
        latent_raw, latent_scale, grad_shard[:, D : D + KV_RANK]
    )
    grad_rope = rotate(
        grad_shard[:, D + KV_RANK : D + KV_RANK + QK_ROPE],
        seq_cos[:shard_rows],
        -seq_sin[:shard_rows],
    )
    grad_latent_all = jnp.concatenate([grad_latent_raw, grad_rope], axis=-1).astype(BF)
    grad_latent_local = dot(normed_first, grad_latent_all, ((0,), (0,)))
    grad_normed_first = grad_shard[:, :D] + dot(grad_latent_all, weight_latent, ((1,), (1,)))
    grad_from_mixer, grad_mixer_part = norm_back(input_float, mixer_scale, grad_normed_first)
    grad_input = grad_hidden_state + grad_from_mixer
    gain_rows = D // KV_RANK
    latent_part = jnp.pad(
        grad_latent_part.reshape(count, KV_RANK // count),
        ((0, 0), (0, (gain_rows - 1) * KV_RANK // count)),
    ).reshape(D, 1)
    small_terms = jnp.concatenate(
        [
            grad_latent_local,
            grad_mixer_part[:, None],
            grad_experts_part[:, None],
            latent_part,
            jnp.zeros((D, latent_pad - KV_RANK - QK_ROPE - 3), F32),
        ],
        axis=1,
    ).astype(BF)
    for k in range(3, len(order_a)):
        result_lower, result_sent, _ = halve_stage(
            result_lower, result_sent, [turn[k] for turn in turns], count
        )
    result = jnp.concatenate(
        [a.astype(F32) + b.astype(F32) for a, b in zip(result_lower, result_sent)], axis=1
    )
    small_terms = jnp.take(small_terms.reshape(count, D // count, latent_pad), group_ids, axis=0)
    small_grads = scatter_rows(small_terms.reshape(D, latent_pad), (CORE,) + order_a[::-1], count)
    at = KV_RANK + QK_ROPE
    grad_latent_weight = small_grads[:, :at]
    grad_attention_gain = small_grads[:, at]
    grad_experts_gain = small_grads[:, at + 1]
    grad_latent_gain = small_grads[: KV_RANK // count, at + 2]
    layer_output = (hidden_late + result).astype(BF)
    return (
        layer_output,
        grad_input,
        grad_attention_gain,
        grad_query_weight,
        grad_latent_weight,
        grad_latent_gain,
        grad_latent_up,
        grad_output_weight,
        grad_experts_gain,
        grad_expert_gate,
        grad_expert_up,
        grad_expert_down,
        grad_shared_gate,
        grad_shared_up,
        grad_shared_down,
    )


def solution(mesh):
    return jax.shard_map(
        local,
        mesh=mesh,
        in_specs=(
            P(("dp", "tensor"), None),
            P("dp", None),
            P(("dp", "tensor"), None),
            P(("dp", "tensor"), None),
            P(("dp", "tensor"), None),
            P("dp"),
            P("dp", "tensor"),
            P("dp", None),
            P("dp"),
            P("dp", "tensor"),
            P("tensor", "dp"),
            P("dp"),
            P("dp", None, "tensor"),
            P("dp", None, "tensor"),
            P("dp", "tensor", None),
            P("dp", None),
            P("dp", None),
            P(None, "dp"),
            P(("dp", "tensor"), None),
        ),
        out_specs=(
            P(("dp", "tensor"), None),
            P(("dp", "tensor"), None),
            P(("dp", "tensor")),
            P("dp", "tensor"),
            P(("dp", "tensor"), None),
            P(("dp", "tensor")),
            P("dp", "tensor"),
            P("tensor", "dp"),
            P(("dp", "tensor")),
            P("dp", None, "tensor"),
            P("dp", None, "tensor"),
            P("dp", "tensor", None),
            P("dp", "tensor"),
            P("dp", "tensor"),
            P("tensor", "dp"),
        ),
        check_vma=False,
    )
```

```python
import functools

import jax
import jax.numpy as jnp
from jax import lax
from jax.experimental import pallas as pl
from jax.experimental.pallas import tpu as pltpu
from jax.sharding import PartitionSpec as P

D = 2048
QK_NOPE = 128
QK_ROPE = 64
V_DIM = 128
KV_RANK = 512
TOPK = 6
NORM_EPS = 1e-06

BF = jnp.bfloat16
F32 = jnp.float32
BOTH = ("dp", "tensor")
CORE = 1
GB = 4
LANES = 128
VMEM_CAP = 60 * 1024 * 1024


def round_up(value, step):
    return (value + step - 1) // step * step


def root_norm(values, gain_row):
    factor = lax.rsqrt(jnp.mean(values * values, axis=-1, keepdims=True) + NORM_EPS)
    return values * factor * gain_row


def turn_tables(positions, half_width):
    frequency = 10000.0 ** (-jnp.arange(half_width, dtype=F32) / half_width)
    angles = positions.astype(F32)[:, None] * frequency[None, :]
    return (jnp.cos(angles), jnp.sin(angles))


def rotate(values, cosine, sine_table):
    half_width = values.shape[-1] // 2
    first_half = values[..., :half_width]
    second_half = values[..., half_width:]
    return jnp.concatenate(
        [
            first_half * cosine - second_half * sine_table,
            first_half * sine_table + second_half * cosine,
        ],
        axis=-1,
    )


def dot(left, right, dims=((1,), (0,))):
    return lax.dot_general(left, right, (dims, ((), ())), preferred_element_type=F32)


def swap_with(values, mask, count):
    return lax.ppermute(values, BOTH, [(i, i ^ mask) for i in range(count)])


def cube_gather(block, masks, count):
    for mask in masks:
        block = jnp.concatenate([block, swap_with(block, mask, count)], axis=0)
    return block


def tie(first, second):
    return lax.optimization_barrier((first, second))


def halve_stage(keeps, receiveds, masks, count, follow=()):
    half = keeps[0].shape[0] // 2
    upper = [
        (k[half:].astype(F32) + r[half:].astype(F32)).astype(BF)
        for k, r in zip(keeps, receiveds)
    ]
    first, follow = tie(upper[:2], follow)
    upper = [*first, *upper[2:]]
    sent = [swap_with(value, mask, count) for value, mask in zip(upper, masks)]
    lower = [
        (k[:half].astype(F32) + r[:half].astype(F32)).astype(BF)
        for k, r in zip(keeps, receiveds)
    ]
    return lower, sent, follow


def scatter_rows(partial, masks, count):
    for mask in masks:
        half = partial.shape[0] // 2
        received = swap_with(partial[half:].astype(BF), mask, count)
        partial = partial[:half].astype(F32) + received.astype(F32)
    return partial


def block_order(block, blocks, swapped):
    if not swapped:
        return block
    top, low = block // (blocks // 2), (block // (blocks // 4)) % 2
    return low * (blocks // 2) + top * (blocks // 4) + block % (blocks // 4)


def one_hot(slot_row, rows):
    tokens = lax.broadcasted_iota(jnp.int32, (rows, slot_row.shape[1]), 0)
    return jnp.where(tokens == slot_row, 1.0, 0.0).astype(BF)


def resident(shape):
    return pl.BlockSpec(shape, lambda *_: (0,) * len(shape), pipeline_mode=pl.Buffered(1))


def cotangent_rows(ids, slot_rows, slot_weights, cotangents, down_t, common_down_t):
    groups, _, slots = slot_rows.shape
    experts, _, width = down_t.shape
    cap = slots // experts
    rows = cotangents.shape[0] // groups
    units = common_down_t.shape[1]

    def body(ids_ref, slot_ref, weight_ref, g0, g1, g2, g3, down_ref, common_ref, rows_ref, dh_ref, dhs_ref):
        for k, g_ref in enumerate((g0, g1, g2, g3)):
            value = g_ref[...]
            picked = dot(one_hot(slot_ref[k], rows), value, ((0,), (0,))).astype(BF)
            for j in range(experts):
                rows_ref[j, k * cap : (k + 1) * cap, :] = picked[j * cap : (j + 1) * cap]
            dhs_ref[k * rows : (k + 1) * rows, :] = dot(value, common_ref[...])
        for j in range(experts):
            dh_ref[j] = dot(rows_ref[j], down_ref[j]) * weight_ref[j][:, :1]

    def row_block(k):
        return pl.BlockSpec((rows, D), lambda i, ids: (ids[GB * i + k], 0))

    return pl.pallas_call(
        body,
        grid_spec=pltpu.PrefetchScalarGridSpec(
            num_scalar_prefetch=1,
            grid=(groups // GB,),
            in_specs=[
                pl.BlockSpec((GB, 1, slots), lambda i, ids: (i, 0, 0)),
                pl.BlockSpec((experts, GB * cap, LANES), lambda i, ids: (0, i, 0)),
                *[row_block(k) for k in range(GB)],
                resident(down_t.shape),
                resident(common_down_t.shape),
            ],
            out_specs=[
                pl.BlockSpec((experts, GB * cap, D), lambda i, ids: (0, i, 0)),
                pl.BlockSpec((experts, GB * cap, width), lambda i, ids: (0, i, 0)),
                pl.BlockSpec((GB * rows, units), lambda i, ids: (i, 0)),
            ],
        ),
        out_shape=[
            jax.ShapeDtypeStruct((experts, groups * cap, D), BF),
            jax.ShapeDtypeStruct((experts, groups * cap, width), F32),
            jax.ShapeDtypeStruct((groups * rows, units), F32),
        ],
        compiler_params=pltpu.CompilerParams(vmem_limit_bytes=VMEM_CAP),
        name="cotangent_rows",
    )(ids, slot_rows, slot_weights, *([cotangents] * GB), down_t, common_down_t)


def expert_hidden(half, streams, order_flags, slot_rows, slot_weights, dh, dhs, weights, previous):
    gate_up, common_t = weights
    groups, _, slots = slot_rows.shape
    experts, _, double = gate_up.shape
    width = double // 2
    cap = slots // experts
    blocks = groups // (2 * GB)
    rows = streams[0].shape[0] // (groups // 2)
    part = streams[0].shape[1]
    units = dhs.shape[1]
    count = len(streams)

    def body(*refs):
        slot_ref, weight_ref, dh_ref, dhs_ref = refs[:4]
        token_refs = refs[4 : 4 + count]
        gu_ref, common_t_ref = refs[4 + count : 6 + count]
        x_ref, hidden_ref, dgu_ref, hs_ref, dgs_ref = refs[-5:]
        for k in range(GB):
            picks = one_hot(slot_ref[k], rows)
            for s in range(count):
                picked = dot(
                    picks, token_refs[s][k * rows : (k + 1) * rows, :], ((0,), (0,))
                ).astype(BF)
                for j in range(experts):
                    x_ref[j, k * cap : (k + 1) * cap, s * part : (s + 1) * part] = picked[
                        j * cap : (j + 1) * cap
                    ]
        common_gu = dot(token_refs[0][...], common_t_ref[:part, :])
        for s in range(1, count):
            common_gu += dot(token_refs[s][...], common_t_ref[s * part : (s + 1) * part, :])
        gate, up = common_gu[:, :units], common_gu[:, units:]
        logistic = jax.nn.sigmoid(gate)
        silu = gate * logistic
        hs_ref[...] = (silu * up).astype(BF)
        grad_hidden = dhs_ref[...]
        slope = logistic * (1.0 + gate * (1.0 - logistic))
        dgs_ref[:, :units] = (grad_hidden * up * slope).astype(BF)
        dgs_ref[:, units:] = (grad_hidden * silu).astype(BF)
        for j in range(experts):
            both = dot(x_ref[j], gu_ref[j])
            gate, up = both[:, :width], both[:, width:]
            logistic = jax.nn.sigmoid(gate)
            silu = gate * logistic
            hidden_ref[j] = (silu * up * weight_ref[j][:, :1]).astype(BF)
            grad_hidden = dh_ref[j]
            slope = logistic * (1.0 + gate * (1.0 - logistic))
            dgu_ref[j, :, :width] = (grad_hidden * up * slope).astype(BF)
            dgu_ref[j, :, width:] = (grad_hidden * silu).astype(BF)

    shift = half * blocks
    token_specs = [
        pl.BlockSpec((GB * rows, part), functools.partial(lambda f, i: (block_order(i, blocks, f), 0), flag))
        for flag in order_flags
    ]
    in_specs = [
        pl.BlockSpec((GB, 1, slots), lambda i: (shift + i, 0, 0)),
        pl.BlockSpec((experts, GB * cap, LANES), lambda i: (0, shift + i, 0)),
        pl.BlockSpec((experts, GB * cap, width), lambda i: (0, shift + i, 0)),
        pl.BlockSpec((GB * rows, units), lambda i: (shift + i, 0)),
        *token_specs,
        resident(gate_up.shape),
        resident(common_t.shape),
    ]
    operands = [slot_rows, slot_weights, dh, dhs, *streams, gate_up, common_t]
    aliases = {}
    if previous is not None:
        for at, value in enumerate(previous):
            aliases[len(operands)] = at
            in_specs.append(pl.BlockSpec(memory_space=pl.ANY))
            operands.append(value)
    return pl.pallas_call(
        body,
        grid=(blocks,),
        in_specs=in_specs,
        out_specs=[
            pl.BlockSpec((experts, GB * cap, D), lambda i: (0, shift + i, 0)),
            pl.BlockSpec((experts, GB * cap, width), lambda i: (0, shift + i, 0)),
            pl.BlockSpec((experts, GB * cap, double), lambda i: (0, shift + i, 0)),
            pl.BlockSpec((GB * rows, units), lambda i: (shift + i, 0)),
            pl.BlockSpec((GB * rows, 2 * units), lambda i: (shift + i, 0)),
        ],
        out_shape=[
            jax.ShapeDtypeStruct((experts, groups * cap, D), BF),
            jax.ShapeDtypeStruct((experts, groups * cap, width), BF),
            jax.ShapeDtypeStruct((experts, groups * cap, double), BF),
            jax.ShapeDtypeStruct((groups * rows, units), BF),
            jax.ShapeDtypeStruct((groups * rows, 2 * units), BF),
        ],
        input_output_aliases=aliases,
        compiler_params=pltpu.CompilerParams(vmem_limit_bytes=VMEM_CAP),
        name="expert_hidden",
    )(*operands)


def token_terms(half, order_flags, slot_rows, slot_values, weights, extra, extra_weights):
    groups, _, slots = slot_rows.shape
    experts, _, width = slot_values.shape
    cap = slots // experts
    rows = extra.shape[0] // groups
    units = extra.shape[1]
    blocks = groups // (2 * GB)
    shift = half * blocks
    count = len(order_flags)
    part = D // count

    def body(slot_ref, value_ref, weight_ref, extra_ref, extra_weight_ref, *out_refs):
        results = [dot(value_ref[j], weight_ref[j]).astype(BF) for j in range(experts)]
        for k in range(GB):
            stacked = jnp.concatenate([r[k * cap : (k + 1) * cap] for r in results], axis=0)
            total = dot(one_hot(slot_ref[k], rows), stacked) + dot(
                extra_ref[k * rows : (k + 1) * rows, :], extra_weight_ref[...]
            )
            for s in range(count):
                out_refs[s][k * rows : (k + 1) * rows, :] = total[
                    :, s * part : (s + 1) * part
                ].astype(BF)

    return pl.pallas_call(
        body,
        grid=(blocks,),
        in_specs=[
            pl.BlockSpec((GB, 1, slots), lambda i: (shift + i, 0, 0)),
            pl.BlockSpec((experts, GB * cap, width), lambda i: (0, shift + i, 0)),
            resident(weights.shape),
            pl.BlockSpec((GB * rows, units), lambda i: (shift + i, 0)),
            resident(extra_weights.shape),
        ],
        out_specs=[
            pl.BlockSpec(
                (GB * rows, part),
                functools.partial(lambda f, i: (block_order(i, blocks, f), 0), flag),
            )
            for flag in order_flags
        ],
        out_shape=[
            jax.ShapeDtypeStruct((groups // 2 * rows, part), BF) for _ in order_flags
        ],
        compiler_params=pltpu.CompilerParams(vmem_limit_bytes=VMEM_CAP),
        name="token_terms",
    )(slot_rows, slot_values, weights, extra, extra_weights)


def slot_tables(routes, route_weight, place_order, expert_total, capacity, padded):
    shard_rows = routes.shape[0]
    pair_count = shard_rows * TOPK
    expert_ids = routes.reshape(pair_count)
    ranks = place_order[0]
    earlier = (expert_ids[:, None] == expert_ids[None, :]) & (ranks[None, :] < ranks[:, None])
    places = jnp.sum(earlier.astype(jnp.int32), axis=1)
    slots = jnp.where(places < capacity, expert_ids * padded + places, -1)
    chosen = slots[:, None] == jnp.arange(expert_total * padded, dtype=jnp.int32)[None, :]
    pair_tokens = (jnp.arange(pair_count, dtype=jnp.int32) // TOPK).astype(F32)
    tokens = shard_rows + jnp.sum(
        jnp.where(chosen, pair_tokens[:, None] - shard_rows, 0.0), axis=0
    )
    weights = jnp.sum(jnp.where(chosen, route_weight.reshape(pair_count)[:, None], 0.0), axis=0)
    return jnp.stack([tokens, weights])


def norm_back(values, gain_row, grads):
    factor = lax.rsqrt(jnp.mean(values * values, axis=-1, keepdims=True) + NORM_EPS)
    scaled = gain_row * grads
    inner = jnp.mean(values * scaled, axis=-1, keepdims=True)
    grad_values = factor * scaled - values * (factor * factor * factor) * inner
    grad_gain = jnp.sum(grads * values * factor, axis=0)
    return grad_values, grad_gain


def local(
    layer_input,
    segment_ids,
    routes,
    route_weight,
    place_order,
    attention_gain,
    query_weight,
    latent_weight,
    latent_gain,
    latent_up,
    output_weight,
    experts_gain,
    expert_gate,
    expert_up,
    expert_down,
    shared_gate,
    shared_up,
    shared_down,
    out_cotangent,
):
    tensor_count = lax.axis_size("tensor")
    dp_count = lax.axis_size("dp")
    count = tensor_count * dp_count
    dp_at = lax.axis_index("dp")
    tensor_at = lax.axis_index("tensor")
    me = dp_at * tensor_count + tensor_at
    shard_rows = layer_input.shape[0]
    seq_len = segment_ids.shape[1]
    row_block = D // dp_count
    outer = [1 << b for b in range(count.bit_length() - 2, 0, -1)]
    order_a = tuple(outer)
    order_b = tuple(outer[:-2] + [outer[-1], outer[-2]])
    stream_orders = (order_a, order_b, order_a, order_b)
    order_flags = (False, True, False, True)
    part = D // len(stream_orders)
    tensor_masks = tuple(1 << b for b in range(tensor_count.bit_length() - 2, -1, -1))

    up_split = row_block // latent_up.shape[0]
    latent_pad = round_up(KV_RANK + QK_ROPE + 3, LANES)
    extras = jnp.concatenate(
        [
            latent_weight,
            attention_gain[:, None],
            experts_gain[:, None],
            jnp.broadcast_to(latent_gain[:, None], (latent_gain.shape[0], up_split)).reshape(-1, 1),
            jnp.zeros((row_block, latent_pad - KV_RANK - QK_ROPE - 3), BF),
        ],
        axis=1,
    )
    query_cols = query_weight.shape[1]
    out_cols = output_weight.shape[0]
    up_cols = latent_up.shape[1] // up_split
    packed = jnp.concatenate(
        [query_weight, output_weight.T, latent_up.reshape(row_block, up_cols), extras], axis=1
    )
    packed_full = lax.all_gather(packed, "dp", axis=0, tiled=True)
    hidden_total = shared_gate.shape[1]
    unit_block = hidden_total // tensor_count
    units = unit_block // dp_count
    unit_pad = round_up(units, LANES)
    column = tensor_at * unit_block
    common_send = jnp.stack(
        [
            lax.dynamic_slice_in_dim(shared_gate, column, unit_block, 1).T,
            lax.dynamic_slice_in_dim(shared_up, column, unit_block, 1).T,
            lax.dynamic_slice_in_dim(shared_down, column, unit_block, 0),
        ]
    ).reshape(3, dp_count, units, row_block)
    common_here = lax.all_to_all(
        jnp.transpose(common_send, (1, 0, 2, 3)), "dp", split_axis=0, concat_axis=0, tiled=True
    )
    common_here = jnp.transpose(common_here, (1, 2, 0, 3)).reshape(3, units, D)
    common_here = jnp.pad(common_here, ((0, 0), (0, unit_pad - units), (0, 0)))
    common_gu = common_here[:2].reshape(2 * unit_pad, D)
    common_down = common_here[2]
    common_gu_t = common_gu.T
    common_down_t = common_down.T

    expert_local = expert_gate.shape[0]
    expert_total = expert_local * dp_count
    capacity = max(2, 5 * shard_rows * TOPK // (4 * expert_total))
    padded = round_up(capacity, 16)
    slots = expert_local * padded
    tables = slot_tables(routes, route_weight, place_order, expert_total, capacity, padded)
    tables_all = cube_gather(tables[None], order_a + (CORE,), count)
    tables_mine = lax.dynamic_slice_in_dim(tables_all, dp_at * slots, slots, 2)
    relative = jnp.zeros((count,), jnp.int32)
    canon = jnp.arange(count, dtype=jnp.int32)
    for bit, mask in enumerate(order_a + (CORE,)):
        relative = relative + mask * ((canon >> bit) & 1)
    group_ids = me ^ relative
    slot_rows = tables_mine[:, :1, :].astype(jnp.int32)
    slot_weights = jnp.transpose(
        tables_mine[:, 1, :].reshape(count, expert_local, padded), (1, 0, 2)
    ).reshape(expert_local, count * padded, 1)
    slot_weights = jnp.broadcast_to(slot_weights, (expert_local, count * padded, LANES))

    width = expert_gate.shape[2]
    width_pad = round_up(width, LANES)
    pad_columns = ((0, 0), (0, 0), (0, width_pad - width))
    gate_up = jnp.concatenate(
        [jnp.pad(expert_gate, pad_columns), jnp.pad(expert_up, pad_columns)], axis=2
    )
    gate_up_t = jnp.transpose(gate_up, (0, 2, 1))
    down_pad = jnp.pad(expert_down, ((0, 0), (0, width_pad - width), (0, 0)))
    down_t = jnp.transpose(down_pad, (0, 2, 1))

    input_seq = cube_gather(layer_input, tensor_masks, count)
    ready = (gate_up, gate_up_t, down_pad, down_t, common_gu, common_gu_t, common_down, common_down_t)
    packed_full, (ready, slot_rows, slot_weights, input_seq) = tie(
        packed_full, (ready, slot_rows, slot_weights, input_seq)
    )
    gate_up, gate_up_t, down_pad, down_t, common_gu, common_gu_t, common_down, common_down_t = ready
    at = query_cols
    weight_query = packed_full[:, :at]
    weight_out_t = packed_full[:, at : at + out_cols]
    at += out_cols
    weight_up = packed_full[:, at : at + up_cols].reshape(KV_RANK, up_split * up_cols)
    at += up_cols
    weight_latent = packed_full[:, at : at + KV_RANK + QK_ROPE]
    at += KV_RANK + QK_ROPE
    mixer_scale = packed_full[:, at].astype(F32)
    experts_scale = packed_full[:, at + 1].astype(F32)
    latent_scale = packed_full[:, at + 2].reshape(KV_RANK, up_split)[:, 0].astype(F32)

    input_float = layer_input.astype(F32)
    hops = jnp.zeros((tensor_count,), jnp.int32)
    seq_blocks = jnp.arange(tensor_count, dtype=jnp.int32)
    for bit, mask in enumerate(tensor_masks):
        hops = hops + mask * ((seq_blocks >> bit) & 1)
    block_ids = tensor_at ^ hops
    positions = (
        block_ids[:, None] * shard_rows + jnp.arange(shard_rows, dtype=jnp.int32)[None, :]
    ).reshape(seq_len)
    doc_ids = jnp.take(segment_ids[0].reshape(tensor_count, shard_rows), block_ids, axis=0)
    doc_ids = doc_ids.reshape(seq_len)
    seq_cos, seq_sin = turn_tables(positions, QK_ROPE // 2)
    normed_full = root_norm(input_seq.astype(F32), mixer_scale).astype(BF)
    normed_first = normed_full[:shard_rows]
    latent_all = dot(normed_full, weight_latent)
    latent_full = root_norm(latent_all[:, :KV_RANK], latent_scale).astype(BF)
    rope_full = rotate(latent_all[:, KV_RANK:], seq_cos, seq_sin).astype(BF)
    latent_raw = latent_all[:shard_rows, :KV_RANK]
    head_dim = QK_NOPE + QK_ROPE
    local_heads = query_cols // head_dim
    query_raw = dot(normed_full, weight_query).reshape(seq_len, local_heads, head_dim)
    query_cat = jnp.concatenate(
        [
            query_raw[..., :QK_NOPE],
            rotate(query_raw[..., QK_NOPE:], seq_cos[:, None, :], seq_sin[:, None, :]),
        ],
        axis=-1,
    ).astype(BF)
    key_value = dot(latent_full, weight_up).astype(BF)
    key_value = key_value.reshape(seq_len, local_heads, QK_NOPE + V_DIM)
    key_rows = jnp.concatenate(
        [
            key_value[..., :QK_NOPE],
            jnp.broadcast_to(rope_full[:, None, :], (seq_len, local_heads, QK_ROPE)),
        ],
        axis=-1,
    )
    values = key_value[..., QK_NOPE:]
    scaling = head_dim ** (-0.5)
    raw_scores = jnp.einsum("qhd,khd->hqk", query_cat, key_rows, preferred_element_type=F32)
    raw_scores = raw_scores * scaling
    allowed = (doc_ids[:, None] == doc_ids[None, :]) & (positions[None, :] <= positions[:, None])
    masked = jnp.where(allowed[None], raw_scores, -1e30)
    row_max = jnp.max(masked, axis=-1, keepdims=True)
    exp_terms = jnp.exp(masked - row_max)
    row_total = jnp.sum(exp_terms, axis=-1, keepdims=True)
    prob_rows = exp_terms / row_total
    heads_out = jnp.einsum("hqk,khd->qhd", prob_rows.astype(BF), values, preferred_element_type=F32)
    heads_out = heads_out.astype(BF).reshape(seq_len, local_heads * V_DIM)
    mixer_terms = dot(heads_out, weight_out_t, ((1,), (1,)))
    mixer_out = scatter_rows(mixer_terms, tensor_masks[::-1], count)
    hidden_state = input_float + mixer_out
    normed_second = root_norm(hidden_state, experts_scale).astype(BF)

    cotangent_all = lax.all_gather(out_cotangent, BOTH, axis=0, tiled=True)
    grad_rows, grad_hidden, grad_hidden_common = cotangent_rows(
        group_ids, slot_rows, slot_weights, cotangent_all, down_t, common_down_t
    )

    near = [
        cube_gather(normed_second[:, s * part : (s + 1) * part], order, count)
        for s, order in enumerate(stream_orders)
    ]
    far = [swap_with(block, CORE, count) for block in near]
    hidden_weights = (gate_up, common_gu_t)
    kept = None
    for half, streams in ((0, near), (1, far)):
        kept = expert_hidden(
            half, streams, order_flags, slot_rows, slot_weights, grad_hidden,
            grad_hidden_common, hidden_weights, kept,
        )
    rows_in, hidden_rows, grad_gu, hidden_common, grad_common = kept
    far_terms = token_terms(
        1, order_flags, slot_rows, grad_gu, gate_up_t, grad_common, common_gu
    )
    far_received = [swap_with(term, CORE, count) for term in far_terms]
    slot_rows_after, _ = tie(slot_rows, far_terms)
    near_terms = token_terms(
        0, order_flags, slot_rows_after, grad_gu, gate_up_t, grad_common, common_gu
    )

    def common_gradients(cotangents):
        half_rows = count // 2 * shard_rows
        parts = []
        for s, flag in enumerate(order_flags):
            total = 0.0
            for h, tokens in ((0, near[s]), (1, far[s])):
                grads = cotangents[h * half_rows : (h + 1) * half_rows]
                if flag:
                    shape = (2, 2, half_rows // 4, 2 * unit_pad)
                    grads = jnp.swapaxes(grads.reshape(shape), 0, 1).reshape(half_rows, 2 * unit_pad)
                total = total + dot(grads, tokens, ((0,), (0,)))
            parts.append(total)
        return jnp.concatenate(parts, axis=1)

    def common_down_gradient(hidden, cotangents):
        canon_ids = jnp.zeros((count,), jnp.int32)
        offset = me ^ canon
        for bit, mask in enumerate(order_a + (CORE,)):
            canon_ids = canon_ids + (1 << bit) * ((offset // mask) & 1)
        in_order = jnp.take(hidden.reshape(count, shard_rows, unit_pad), canon_ids, axis=0)
        return dot(in_order.reshape(count * shard_rows, unit_pad), cotangents, ((0,), (0,)))

    if count > 32:
        grad_common_gu = common_gradients(grad_common)
        near_terms, grad_common_gu = tie(near_terms, grad_common_gu)
    turns = [order[::-1] for order in stream_orders]

    lower, sent, (slot_rows_late, rows_late, grad_gu_late, hidden_late) = halve_stage(
        near_terms, far_received, [turn[0] for turn in turns], count,
        (slot_rows, rows_in, grad_gu, hidden_rows),
    )

    def result_exchange(slot_rows_late):
        far_results = token_terms(
            1, order_flags, slot_rows_late, hidden_late, down_pad, hidden_common, common_down
        )
        far_results, slot_rows_late = tie(far_results, slot_rows_late)
        far_results_received = [swap_with(term, CORE, count) for term in far_results]
        near_results = token_terms(
            0, order_flags, slot_rows_late, hidden_late, down_pad, hidden_common, common_down
        )
        return near_results, far_results_received

    grad_expert_gate = jnp.stack(
        [dot(rows_late[j], grad_gu_late[j, :, :width], ((0,), (0,))) for j in range(expert_local)]
    )
    if count <= 32:
        near_results, far_results_received = result_exchange(slot_rows_late)
    lower, sent, (rows_late, grad_gu_late, hidden_late, grad_common_late) = halve_stage(
        lower, sent, [turn[1] for turn in turns], count,
        (rows_late, grad_gu_late, hidden_late, grad_common),
    )
    grad_expert_up = jnp.stack(
        [
            dot(rows_late[j], grad_gu_late[j, :, width_pad : width_pad + width], ((0,), (0,)))
            for j in range(expert_local)
        ]
    )
    if count <= 32:
        lower, sent, (near_results, hidden_late, grad_common_late) = halve_stage(
            lower, sent, [turn[2] for turn in turns], count,
            (near_results, hidden_late, grad_common_late),
        )
        grad_common_gu = common_gradients(grad_common_late)
        grad_common_down = common_down_gradient(hidden_common, cotangent_all)
        result_lower, result_sent, _ = halve_stage(
            near_results, far_results_received, [turn[0] for turn in turns], count
        )
    else:
        lower, sent, _ = halve_stage(lower, sent, [turn[2] for turn in turns], count)
    for k in range(3, len(order_a)):
        lower, sent, _ = halve_stage(lower, sent, [turn[k] for turn in turns], count)
    grad_normed_second = jnp.concatenate(
        [a.astype(F32) + b.astype(F32) for a, b in zip(lower, sent)], axis=1
    )
    grad_expert_down = jnp.stack(
        [dot(hidden_late[j][:, :width], grad_rows[j], ((0,), (0,))) for j in range(expert_local)]
    )

    if count > 32:
        again, grad_normed_second = tie(out_cotangent, grad_normed_second)
        cotangent_all = lax.all_gather(again, BOTH, axis=0, tiled=True)
        grad_common_down = common_down_gradient(hidden_common, cotangent_all)
    common_grads = jnp.stack(
        [grad_common_gu[:units], grad_common_gu[unit_pad : unit_pad + units], grad_common_down[:units]]
    ).astype(BF)
    common_grads = jnp.transpose(
        common_grads.reshape(3, units, dp_count, row_block), (2, 0, 1, 3)
    )
    common_grads = lax.all_to_all(common_grads, "dp", split_axis=0, concat_axis=0, tiled=True)
    common_grads = jnp.transpose(common_grads, (1, 0, 2, 3)).reshape(3, unit_block, row_block)
    grad_shared_gate = common_grads[0].T.astype(F32)
    grad_shared_up = common_grads[1].T.astype(F32)
    grad_shared_down = common_grads[2].astype(F32)

    if count > 32:
        slot_rows_late, grad_normed_second = tie(slot_rows_late, grad_normed_second)
        near_results, far_results_received = result_exchange(slot_rows_late)
        result_lower, result_sent, _ = halve_stage(
            near_results, far_results_received, [turn[0] for turn in turns], count
        )
    cotangent = out_cotangent.astype(F32)
    grad_from_experts, grad_experts_part = norm_back(hidden_state, experts_scale, grad_normed_second)
    grad_hidden_state = cotangent + grad_from_experts
    grad_mixer_full = cube_gather(grad_hidden_state.astype(BF), tensor_masks, count)
    grad_output_t = dot(grad_mixer_full, heads_out, ((0,), (0,)))
    result_lower, result_sent, _ = halve_stage(
        result_lower, result_sent, [turn[1] for turn in turns], count
    )
    grad_output_t = lax.psum_scatter(
        grad_output_t.astype(BF), "dp", scatter_dimension=0, tiled=True
    )
    grad_heads = dot(grad_mixer_full, weight_out_t).astype(BF)
    grad_heads = grad_heads.reshape(seq_len, local_heads, V_DIM)
    grad_probs = jnp.einsum("qhd,khd->hqk", grad_heads, values, preferred_element_type=F32)
    row_dot = jnp.sum(prob_rows * grad_probs, axis=-1, keepdims=True)
    grad_scores = (prob_rows * (grad_probs - row_dot)).astype(BF)
    grad_query = scaling * jnp.einsum(
        "hqk,khd->qhd", grad_scores, key_rows, preferred_element_type=F32
    )
    grad_keys = scaling * jnp.einsum(
        "hqk,qhd->khd", grad_scores, query_cat, preferred_element_type=F32
    )
    grad_values = jnp.einsum(
        "hqk,qhd->khd", prob_rows.astype(BF), grad_heads, preferred_element_type=F32
    )
    grad_query_raw = (
        jnp.concatenate(
            [
                grad_query[..., :QK_NOPE],
                rotate(grad_query[..., QK_NOPE:], seq_cos[:, None, :], -seq_sin[:, None, :]),
            ],
            axis=-1,
        )
        .reshape(seq_len, local_heads * head_dim)
        .astype(BF)
    )
    grad_key_value = (
        jnp.concatenate([grad_keys[..., :QK_NOPE], grad_values], axis=-1)
        .reshape(seq_len, local_heads * (QK_NOPE + V_DIM))
        .astype(BF)
    )
    grad_terms = jnp.concatenate(
        [
            dot(grad_query_raw, weight_query, ((1,), (1,))).astype(BF),
            dot(grad_key_value, weight_up, ((1,), (1,))).astype(BF),
            jnp.sum(grad_keys[..., QK_NOPE:], axis=1).astype(BF),
            jnp.zeros((seq_len, QK_ROPE), BF),
        ],
        axis=1,
    )
    grad_shard = scatter_rows(grad_terms, tensor_masks[::-1], count)
    grad_shard, hidden_late = tie(grad_shard, hidden_state)
    result_lower, result_sent, _ = halve_stage(
        result_lower, result_sent, [turn[2] for turn in turns], count
    )
    grad_query_local = dot(normed_full, grad_query_raw, ((0,), (0,)))
    grad_up_local = dot(latent_full, grad_key_value, ((0,), (0,)))
    weight_terms = jnp.concatenate(
        [
            grad_query_local.astype(BF),
            grad_up_local.astype(BF).reshape(D, up_cols),
        ],
        axis=1,
    )
    weight_grads = lax.psum_scatter(weight_terms, "dp", scatter_dimension=0, tiled=True)
    weight_grads = weight_grads.astype(F32)
    grad_query_weight = weight_grads[:, :query_cols]
    grad_output_weight = grad_output_t.astype(F32).T
    grad_latent_up = weight_grads[:, query_cols:].reshape(latent_up.shape)

    grad_latent_raw, grad_latent_part = norm_back(
        latent_raw, latent_scale, grad_shard[:, D : D + KV_RANK]
    )
    grad_rope = rotate(
        grad_shard[:, D + KV_RANK : D + KV_RANK + QK_ROPE],
        seq_cos[:shard_rows],
        -seq_sin[:shard_rows],
    )
    grad_latent_all = jnp.concatenate([grad_latent_raw, grad_rope], axis=-1).astype(BF)
    grad_latent_local = dot(normed_first, grad_latent_all, ((0,), (0,)))
    grad_normed_first = grad_shard[:, :D] + dot(grad_latent_all, weight_latent, ((1,), (1,)))
    grad_from_mixer, grad_mixer_part = norm_back(input_float, mixer_scale, grad_normed_first)
    grad_input = grad_hidden_state + grad_from_mixer
    gain_rows = D // KV_RANK
    latent_part = jnp.pad(
        grad_latent_part.reshape(count, KV_RANK // count),
        ((0, 0), (0, (gain_rows - 1) * KV_RANK // count)),
    ).reshape(D, 1)
    small_terms = jnp.concatenate(
        [
            grad_latent_local,
            grad_mixer_part[:, None],
            grad_experts_part[:, None],
            latent_part,
            jnp.zeros((D, latent_pad - KV_RANK - QK_ROPE - 3), F32),
        ],
        axis=1,
    ).astype(BF)
    for k in range(3, len(order_a)):
        result_lower, result_sent, _ = halve_stage(
            result_lower, result_sent, [turn[k] for turn in turns], count
        )
    result = jnp.concatenate(
        [a.astype(F32) + b.astype(F32) for a, b in zip(result_lower, result_sent)], axis=1
    )
    small_terms = jnp.take(small_terms.reshape(count, D // count, latent_pad), group_ids, axis=0)
    small_grads = scatter_rows(small_terms.reshape(D, latent_pad), (CORE,) + order_a[::-1], count)
    at = KV_RANK + QK_ROPE
    grad_latent_weight = small_grads[:, :at]
    grad_attention_gain = small_grads[:, at]
    grad_experts_gain = small_grads[:, at + 1]
    grad_latent_gain = small_grads[: KV_RANK // count, at + 2]
    layer_output = (hidden_late + result).astype(BF)
    return (
        layer_output,
        grad_input,
        grad_attention_gain,
        grad_query_weight,
        grad_latent_weight,
        grad_latent_gain,
        grad_latent_up,
        grad_output_weight,
        grad_experts_gain,
        grad_expert_gate,
        grad_expert_up,
        grad_expert_down,
        grad_shared_gate,
        grad_shared_up,
        grad_shared_down,
    )


def solution(mesh):
    return jax.shard_map(
        local,
        mesh=mesh,
        in_specs=(
            P(("dp", "tensor"), None),
            P("dp", None),
            P(("dp", "tensor"), None),
            P(("dp", "tensor"), None),
            P(("dp", "tensor"), None),
            P("dp"),
            P("dp", "tensor"),
            P("dp", None),
            P("dp"),
            P("dp", "tensor"),
            P("tensor", "dp"),
            P("dp"),
            P("dp", None, "tensor"),
            P("dp", None, "tensor"),
            P("dp", "tensor", None),
            P("dp", None),
            P("dp", None),
            P(None, "dp"),
            P(("dp", "tensor"), None),
        ),
        out_specs=(
            P(("dp", "tensor"), None),
            P(("dp", "tensor"), None),
            P(("dp", "tensor")),
            P("dp", "tensor"),
            P(("dp", "tensor"), None),
            P(("dp", "tensor")),
            P("dp", "tensor"),
            P("tensor", "dp"),
            P(("dp", "tensor")),
            P("dp", None, "tensor"),
            P("dp", None, "tensor"),
            P("dp", "tensor", None),
            P("dp", "tensor"),
            P("dp", "tensor"),
            P("tensor", "dp"),
        ),
        check_vma=False,
    )
```
